32 devices in a mesh: ctx: 8 (over y, x, core), head: 4 (over z).
Axes of the slice: x: 2, y: 2, z: 4, core: 2. Of those that a mesh axis runs over, the one named last changes fastest.
Arguments:
- queries: bfloat16 [2048, 4096], P(('ctx', 'head')), may hold values from -0.59765625 to 0.59765625
- key_in: bfloat16 [2048, 4096], P(('ctx', 'head')), may hold values from -0.59765625 to 0.59765625
- values_in: bfloat16 [2048, 4096], P(('ctx', 'head')), may hold values from -6 to 6
- strength: bfloat16 [2048, 32], P(('ctx', 'head')), may hold values from 0 to 0.95, as said below
- log_decay: bfloat16 [2048, 4096], P(('ctx', 'head')), may hold values from -1.2 to 0, as said below
- d_out: bfloat16 [2048, 4096], P(('ctx', 'head')), may hold values from -6 to 6
Outputs:
- d_queries: bfloat16 [2048, 4096], P(('ctx', 'head'))
- d_keys: bfloat16 [2048, 4096], P(('ctx', 'head'))
- d_values: bfloat16 [2048, 4096], P(('ctx', 'head'))
- d_strength: bfloat16 [2048, 32], P(('ctx', 'head'))
- d_log_decay: bfloat16 [2048, 4096], P(('ctx', 'head'))
The draws below stay inside these ranges and needn't reach their ends.
Inputs may be any that keep to these rules, and one draw needn't show every extreme that they name: `log_decay`: every log decay is negative. Every write strength is positive and below one.
All inputs are finite; a program needn't handle non-finite values.
Results may differ from the reference program's by a relative error of at most 0.00215.
Values may be sent and summed in bfloat16 or wider, within the bound.
A program may use at most 128 MiB of HBM per device.

```python
import jax
import jax.numpy as jnp
from jax import lax

HEADS = 32
HEAD_DIM = 128
SPAN = 64
TOK_CTX = 256
TOKENS = 2048


def draw_strength(key, part):
    shards = TOKENS // TOK_CTX
    pick_key, strong_key, weak_key, block_key, rough_key = jax.random.split(key, 5)
    share = 3
    strong_head = jax.random.randint(pick_key, (HEADS,), 0, 8) < share
    strong_value = jax.random.uniform(strong_key, (TOKENS, HEADS), jnp.float32, 0.2, 0.95)
    weak_base = jnp.exp(jax.random.uniform(weak_key, (HEADS,), jnp.float32, jnp.log(0.1), jnp.log(1.5))) * (HEAD_DIM / TOKENS)
    block_factor = jnp.exp(jax.random.uniform(block_key, (shards, 1, HEADS), jnp.float32, -0.7, 0.7))
    rough_factor = jnp.exp(jax.random.uniform(rough_key, (shards, TOK_CTX, HEADS), jnp.float32, -0.7, 0.7))
    weak_value = jnp.minimum((weak_base * block_factor * rough_factor).reshape(TOKENS, HEADS), 0.95)
    return jnp.where(strong_head[None, :], strong_value, weak_value).astype(jnp.bfloat16)


def draw_log_decay(key, part):
    channels = HEADS * HEAD_DIM
    shards = TOKENS // TOK_CTX
    pick_key, fast_key, slow_key, block_key, rough_key, spot_key, cut_key = jax.random.split(key, 7)
    share = 4
    fast_mask = jax.random.randint(pick_key, (channels,), 0, 8) < share
    fast_rate = jnp.exp(jax.random.uniform(fast_key, (channels,), jnp.float32, jnp.log(0.06), jnp.log(0.1)))
    slow_rate = jax.random.uniform(slow_key, (channels,), jnp.float32, 0.1, 1.0) * (1.0 / TOKENS)
    base_rate = jnp.where(fast_mask, fast_rate, slow_rate)
    block_factor = jnp.exp(jax.random.uniform(block_key, (shards, 1, channels), jnp.float32, -0.7, 0.7))
    rough_factor = jnp.exp(jax.random.uniform(rough_key, (shards, TOK_CTX, channels), jnp.float32, -0.7, 0.7))
    rates = (base_rate * block_factor * rough_factor).reshape(TOKENS, channels)
    spots = jax.random.randint(spot_key, (3,), 0, TOKENS)
    struck = jnp.any(jnp.arange(TOKENS)[:, None] == spots[None, :], axis=1)
    cuts = jnp.log(jax.random.uniform(cut_key, (TOKENS, channels), jnp.float32, 0.5, 0.8))
    return (jnp.where(struck[:, None], cuts, 0.0) - rates).astype(jnp.bfloat16)


def block_scale(rng, dims, cuts, least, top_value):
    def one(position, blocks):
        steps = jax.random.uniform(jax.random.fold_in(jax.random.fold_in(rng, 6), position), (blocks,), jnp.float32, least / len(cuts), top_value / len(cuts))
        return jnp.repeat(jnp.exp(steps), dims[position] // blocks).reshape((-1,) + (1,) * (len(dims) - position - 1))

    factor_of = one(*cuts[0])
    for cut in cuts[1:]:
        factor_of = factor_of * one(*cut)
    return factor_of


def gaussian(key, shape, width, bound, cuts=(), held_as=jnp.bfloat16):
    loudness = block_scale(key, shape, cuts, -0.22, 0.18) if cuts else 1.0
    values = jax.random.normal(key, shape, jnp.float32) * width * loudness
    return jnp.minimum(jnp.maximum(values, -bound), bound).astype(held_as)


def setup_inputs(seed: int = 0) -> dict:
    splits = jax.random.split(jax.random.key(seed), 7)
    queries = gaussian(splits[0], (TOKENS, HEADS * HEAD_DIM), 0.088, 0.59765625, ((0, 32),))
    key_in = gaussian(splits[1], (TOKENS, HEADS * HEAD_DIM), 0.088, 0.59765625, ((0, 32),))
    values_in = gaussian(splits[2], (TOKENS, HEADS * HEAD_DIM), 1.0, 6.0, ((0, 32),))
    strength = draw_strength(jax.random.fold_in(splits[6], 71), 0)
    log_decay = draw_log_decay(jax.random.fold_in(splits[6], 71), 0)
    d_out = gaussian(splits[5], (TOKENS, HEADS * HEAD_DIM), 1.0, 6.0, ((0, 32),))
    return {"queries": queries, "key_in": key_in, "values_in": values_in, "strength": strength, "log_decay": log_decay, "d_out": d_out}


exact_prec = lax.Precision.HIGHEST
epsilon = 1e-06

def prepare(queries, keys_used, values_used, strength, log_decay):
    span_len = queries.shape[1]
    head_width = queries.shape[3]
    q_unit = queries * lax.rsqrt(lax.optimization_barrier(jnp.sum(queries * queries, axis=3, keepdims=True)) + epsilon) * head_width ** (-0.5)
    k_unit = keys_used * lax.rsqrt(lax.optimization_barrier(jnp.sum(keys_used * keys_used, axis=3, keepdims=True)) + epsilon)
    gamma = jnp.cumsum(log_decay, axis=1)
    middle = gamma[:, span_len // 2 - 1:span_len // 2]
    q_rise = q_unit * jnp.exp(gamma - middle)
    k_rise = k_unit * jnp.exp(gamma - middle)
    k_fall = k_unit * jnp.exp(middle - gamma)
    strict_mask = jnp.tril(jnp.ones((span_len, span_len), jnp.float32), -1)
    causal_mask = jnp.tril(jnp.ones((span_len, span_len), jnp.float32))
    key_inner = jnp.einsum('ntha,nsha->nhts', k_rise, k_fall, precision=exact_prec) * strict_mask
    scores = jnp.einsum('ntha,nsha->nhts', q_rise, k_fall, precision=exact_prec) * causal_mask
    strength_t = jnp.transpose(strength, (0, 2, 1))
    system = jnp.eye(span_len, dtype=jnp.float32) + strength_t[..., None] * key_inner
    k_head = k_unit * jnp.exp(gamma)
    right_side = jnp.concatenate([values_used, k_head], axis=3) * strength[..., None]
    right_side = jnp.transpose(right_side, (0, 2, 1, 3))
    solved = lax.linalg.triangular_solve(system, right_side, left_side=True, lower=True, unit_diagonal=True)
    w_value = solved[..., :head_width]
    w_key = solved[..., head_width:]
    gamma_end = gamma[:, -1:]
    key_tail = k_unit * jnp.exp(gamma_end - gamma)
    fade_last = jnp.exp(gamma_end[:, 0])
    q_head = q_unit * jnp.exp(gamma)
    return (q_head, scores, w_value, w_key, key_tail, fade_last)

def march(w_value, w_key, key_tail, fade_last, state):

    def advance(state_now, piece_data):
        value_part, key_part, tail_part, fade_part = piece_data
        updates = value_part - jnp.einsum('hta,hab->htb', key_part, state_now, precision=exact_prec)
        following = fade_part[:, :, None] * state_now + jnp.einsum('tha,htb->hab', tail_part, updates, precision=exact_prec)
        return (following, (state_now, updates))
    final_state, (start_states, all_updates) = lax.scan(advance, state, (w_value, w_key, key_tail, fade_last))
    return (final_state, start_states, all_updates)

def sweep(prepared, state):
    q_head, scores, w_value, w_key, key_tail, fade_last = prepared
    final_state, start_states, all_updates = march(w_value, w_key, key_tail, fade_last, state)
    output = jnp.einsum('ntha,nhab->nthb', q_head, start_states, precision=exact_prec)
    output = output + jnp.einsum('nhts,nhsb->nthb', scores, all_updates, precision=exact_prec)
    return (output, final_state)

def reference(queries, key_in, values_in, strength, log_decay, d_out):
    heads_all = strength.shape[1]
    head_width = queries.shape[1] // heads_all
    total = queries.shape[0]
    blocks = total // SPAN

    def by_head(array):
        return jnp.transpose(array.reshape(total, heads_all, head_width), (1, 0, 2))

    def one_head(packed):
        q_one, k_one, v_one, s_one, g_one, o_one = packed

        def shaped(array):
            return array.astype(jnp.float32).reshape(blocks, SPAN, 1, head_width)

        def forward(q_in, k_in, v_in, s_in, g_in):
            prepared = prepare(q_in, k_in, v_in, s_in, g_in)
            return sweep(prepared, jnp.zeros((1, head_width, head_width), jnp.float32))[0]
        strength_one = s_one.astype(jnp.float32).reshape(blocks, SPAN, 1)
        _, pull = jax.vjp(forward, shaped(q_one), shaped(k_one), shaped(v_one), strength_one, shaped(g_one))
        d_q, d_k, d_v, d_s, d_g = pull(shaped(o_one))

        def flatten(array):
            return array.reshape(total, head_width).astype(jnp.bfloat16)
        return (flatten(d_q), flatten(d_k), flatten(d_v), d_s.reshape(total).astype(jnp.bfloat16), flatten(d_g))
    results = lax.map(one_head, (by_head(queries), by_head(key_in), by_head(values_in), jnp.transpose(strength), by_head(log_decay), by_head(d_out)))

    def regather(array):
        return jnp.transpose(array, (1, 0, 2)).reshape(total, heads_all * head_width)
    return (regather(results[0]), regather(results[1]), regather(results[2]), jnp.transpose(results[3]), regather(results[4]))
```

```python
import functools

import jax
import jax.numpy as jnp
from jax import lax
from jax.experimental import pallas as pl
from jax.experimental.pallas import tpu as pltpu
from jax.sharding import PartitionSpec as P

SPAN = 64
BASE = 8
EPS = 1e-06
F32 = jnp.float32
BF16 = jnp.bfloat16
exact_prec = lax.Precision.HIGHEST

NN = (((1,), (0,)), ((), ()))
NT = (((1,), (1,)), ((), ()))


def split(x):
    high = x.astype(BF16)
    return high, (x - high.astype(F32)).astype(BF16)


def mul(a, b, dims=NN):
    return lax.dot_general(a, b, dims, preferred_element_type=F32)


def dot3(a, b, dims=NN):
    if not isinstance(a, tuple):
        return mul(a, b[0], dims) + mul(a, b[1], dims)
    if not isinstance(b, tuple):
        return mul(a[0], b, dims) + mul(a[1], b, dims)
    return mul(a[0], b[0], dims) + (mul(a[0], b[1], dims) + mul(a[1], b[0], dims))


def rows_of(pair, start, size):
    if not isinstance(pair, tuple):
        return pair[start : start + size]
    return tuple(part[start : start + size] for part in pair)


def both(a, b, axis):
    return tuple(jnp.concatenate([x, y], axis=axis) for x, y in zip(a, b))


def grids(size):
    return (
        lax.broadcasted_iota(jnp.int32, (size, size), 0),
        lax.broadcasted_iota(jnp.int32, (size, size), 1),
    )


def per_span(row_values, span, like):
    rows, width = like.shape
    return jnp.broadcast_to(row_values, (rows // span, span, width)).reshape(rows, width)


def gates(g, span):
    rows, width = g.shape
    row, col = grids(rows)
    sum_mask = jnp.where((row // span == col // span) & (col <= row), 1.0, 0.0).astype(BF16)
    gamma = mul(sum_mask, g)
    spans = gamma.reshape(rows // span, span, width)
    middle = spans[:, span // 2 - 1 : span // 2]
    end = spans[:, span - 1 : span]
    centred = gamma - per_span(middle, span, gamma)
    rise = jnp.exp(centred)
    fall = jnp.exp(-centred)
    head = rise * per_span(jnp.exp(middle), span, gamma)
    tail = fall * per_span(jnp.exp(end - middle), span, gamma)
    fade = jnp.exp(end).reshape(rows // span, width)
    return rise, fall, head, tail, fade


def column_of(table, index):
    lane = lax.broadcasted_iota(jnp.int32, table.shape, 1)
    return jnp.sum(jnp.where(lane == index, table, 0.0), axis=1, keepdims=True)


def norm_of(x):
    return lax.rsqrt(jnp.sum(x * x, axis=1, keepdims=True) + EPS)


def inverse(system, row, col):
    same = row // BASE == col // BASE
    near = jnp.where(same, system, 0.0)
    near_s = split(near)
    square = dot3(near_s, near_s)
    square_s = split(square)
    found = jnp.where(row == col, 1.0, 0.0) - near
    fourth = dot3(square_s, square_s)
    found = found + dot3(split(found), square_s)
    found = found + dot3(split(found), split(fourth))
    block = BASE
    while block < SPAN:
        wide = row // (2 * block) == col // (2 * block)
        off = jnp.where(wide & (row // block != col // block), system, 0.0)
        found_s = split(found)
        found = found - dot3(found_s, split(dot3(split(off), found_s)))
        block *= 2
    return found


def local_kernel(span, q_ref, k_ref, v_ref, g_ref, o_ref, b_ref, ev_ref, ek_ref, inv_ref, a_ref, sc_ref,
                 tr_ref, bs_ref, gs_ref, end_ref, trans_ref, inject_ref):
    head_index = pl.program_id(0)
    rows, width = q_ref.shape
    spans = rows // span
    q = q_ref[...].astype(F32)
    k = k_ref[...].astype(F32)
    v = v_ref[...]
    o = o_ref[...]
    beta = column_of(b_ref[...], head_index)
    rise, fall, head, tail, fade = gates(g_ref[...], span)
    q_unit = q * norm_of(q) * width ** (-0.5)
    k_unit = k * norm_of(k)
    row, col = grids(rows)
    inside = row // span == col // span
    k_fall_s = split(k_unit * fall)
    inner = jnp.where(inside & (col < row), dot3(split(k_unit * rise), k_fall_s, NT), 0.0)
    scores = jnp.where(inside & (col <= row), dot3(split(q_unit * rise), k_fall_s, NT), 0.0)
    a_ref[0] = inner
    sc_ref[0] = scores
    beta_row = jnp.sum(jnp.where(row == col, beta, 0.0), axis=0, keepdims=True)
    found = inverse(inner * beta_row, row, col)
    inv_ref[0] = found
    found_s = split(found)
    e_value = dot3(found_s, v)
    e_key = dot3(found_s, split(k_unit * head))
    ev_ref[0] = e_value
    ek_ref[0] = e_key
    w_key_s = split(e_key * beta)
    w_value_s = split(e_value * beta)
    reach = q_unit * head - dot3(split(scores), w_key_s)
    k_tail = k_unit * tail
    small_row, small_col = grids(width)
    diagonal = small_row == small_col
    moves, adds, backs = [], [], []
    for index in range(spans):
        at = index * span
        tail_t = split(k_tail[at : at + span].T)
        move = jnp.where(diagonal, fade[index : index + 1], 0.0) - dot3(tail_t, rows_of(w_key_s, at, span))
        add = dot3(tail_t, rows_of(w_value_s, at, span))
        back = dot3(split(reach[at : at + span].T), o[at : at + span])
        tr_ref[0, index] = move
        bs_ref[0, index] = add
        gs_ref[0, index] = back
        moves.append(move)
        adds.append(add)
        backs.append(back)
    trans, ends = moves[0], adds[0]
    grad = backs[spans - 1]
    for index in range(1, spans):
        move_s = split(moves[index])
        trans = dot3(move_s, split(trans))
        ends = dot3(move_s, split(ends)) + adds[index]
        mirror = spans - 1 - index
        grad = dot3(split(moves[mirror].T), split(grad)) + backs[mirror]
    trans_ref[0] = trans
    end_ref[0] = ends
    inject_ref[0] = grad


def grad_kernel(span, q_ref, k_ref, v_ref, g_ref, o_ref, b_ref, ev_ref, ek_ref, inv_ref, a_ref, sc_ref,
                tr_ref, bs_ref, gs_ref, state_ref, dstate_ref, dq_ref, dk_ref, dv_ref, dg_ref, db_ref):
    head_index = pl.program_id(0)
    rows, width = q_ref.shape
    spans = rows // span
    q = q_ref[...].astype(F32)
    k = k_ref[...].astype(F32)
    o = o_ref[...]
    beta = column_of(b_ref[...], head_index)
    rise, fall, head, tail, fade = gates(g_ref[...], span)
    q_norm = norm_of(q)
    k_norm = norm_of(k)
    q_unit = q * q_norm * width ** (-0.5)
    k_unit = k * k_norm
    row, col = grids(rows)
    inside = row // span == col // span
    states = [state_ref[0]]
    grads = [dstate_ref[0]]
    for index in range(spans - 1):
        states.append(dot3(split(tr_ref[0, index]), split(states[-1])) + bs_ref[0, index])
        mirror = spans - 1 - index
        grads.insert(0, dot3(split(tr_ref[0, mirror].T), split(grads[0])) + gs_ref[0, mirror])
    states_s = [split(x) for x in states]
    grads_s = [split(x) for x in grads]

    def each(fn):
        return jnp.concatenate([fn(index, index * span) for index in range(spans)], axis=0)

    ek_s = split(ek_ref[0])
    k_tail = k_unit * tail
    k_tail_s = split(k_tail)
    error = ev_ref[0] - each(lambda i, at: dot3(rows_of(ek_s, at, span), states_s[i]))
    update_s = split(error * beta)
    d_update = dot3(split(sc_ref[0].T), o) + each(lambda i, at: dot3(rows_of(k_tail_s, at, span), grads_s[i]))
    d_value = dot3(split(inv_ref[0].T), split(d_update * beta))
    d_value_s = split(d_value)
    dv_ref[...] = d_value.astype(BF16)
    residue = d_update - dot3(split(a_ref[0].T), d_value_s)
    d_beta = jnp.sum(error * residue, axis=1, keepdims=True)
    lane = lax.broadcasted_iota(jnp.int32, b_ref.shape, 1)
    db_ref[...] = jnp.where(lane == head_index, d_beta, db_ref[...])
    dq_head = each(lambda i, at: dot3(o[at : at + span], states_s[i], NT))
    dk_head = -each(lambda i, at: dot3(rows_of(d_value_s, at, span), states_s[i], NT))
    dk_tail = each(lambda i, at: dot3(rows_of(update_s, at, span), grads_s[i], NT))
    d_scores = jnp.where(inside & (col <= row), dot3(o, update_s, NT), 0.0)
    d_inner = jnp.where(inside & (col < row), -dot3(d_value_s, update_s, NT), 0.0)
    k_fall_s = split(k_unit * fall)
    dq_rise = dot3(split(d_scores), k_fall_s)
    dk_rise = dot3(split(d_inner), k_fall_s)
    dk_fall = dot3(split(d_scores.T), split(q_unit * rise)) + dot3(split(d_inner.T), split(k_unit * rise))
    dq_unit = dq_rise * rise + dq_head * head
    up = dk_rise * rise + dk_head * head
    tail_part = dk_tail * tail
    down = dk_fall * fall + tail_part
    d_gamma = q_unit * dq_unit + k_unit * (up - down)
    tail_sum = jnp.sum((k_unit * tail_part).reshape(spans, span, width), axis=1, keepdims=True)
    small_row, small_col = grids(width)
    diagonal = small_row == small_col
    last = []
    for index in range(spans):
        d_fade = jnp.sum(states[index] * grads[index], axis=1, keepdims=True)
        d_fade = jnp.sum(jnp.where(diagonal, d_fade, 0.0), axis=0, keepdims=True)
        last.append(d_fade * fade[index : index + 1])
    last = jnp.concatenate([x.reshape(1, 1, width) for x in last], axis=0)
    sum_mask = jnp.where(inside & (col >= row), 1.0, 0.0).astype(BF16)
    d_decay = dot3(sum_mask, split(d_gamma)) + per_span(tail_sum + last, span, d_gamma)
    dg_ref[...] = d_decay.astype(BF16)
    scale = width ** (-0.5)
    dq = (dq_unit - q * (q_norm * q_norm * jnp.sum(q * dq_unit, axis=1, keepdims=True))) * (q_norm * scale)
    dq_ref[...] = dq.astype(BF16)
    dk_unit = up + down
    dk = (dk_unit - k * (k_norm * k_norm * jnp.sum(k * dk_unit, axis=1, keepdims=True))) * k_norm
    dk_ref[...] = dk.astype(BF16)


def passed_along(value, axis, steps):
    count = lax.axis_size(axis)
    leading, last = (max(0, -steps), min(count, count - steps))
    return lax.ppermute(value, axis, [(source, source + steps) for source in range(leading, last)])


def relay(trans, ends, inject):
    n_context = lax.axis_size("ctx")

    def turn(turn_index, carried):
        leaving, back_leaving, _, _ = carried
        arriving = passed_along(leaving, "ctx", 1)
        back_arriving = passed_along(back_leaving, "ctx", -1)
        leaving = jnp.einsum("hab,hbc->hac", trans, arriving, precision=exact_prec) + ends
        back_leaving = jnp.einsum("hba,hbc->hac", trans, back_arriving, precision=exact_prec) + inject
        return (leaving, back_leaving, arriving, back_arriving)

    zero = jnp.zeros_like(ends)
    return lax.fori_loop(0, n_context - 1, turn, (ends, inject, zero, zero))[2:]


def per_device(queries, key_in, values_in, strength, log_decay, d_out):
    heads_all = strength.shape[1]
    heads = heads_all // lax.axis_size("head")
    width = queries.shape[1] // heads_all

    def gathered(array):
        return lax.all_to_all(array, "head", split_axis=1, concat_axis=0, tiled=True)

    k, g, s, q, v, o = (gathered(x) for x in (key_in, log_decay, strength, queries, values_in, d_out))
    s = s.astype(F32)
    rows = q.shape[0]
    spans = rows // SPAN
    token = pl.BlockSpec((rows, width), lambda h: (0, h))
    table = pl.BlockSpec((rows, heads), lambda h: (0, 0))
    narrow = pl.BlockSpec((1, rows, width), lambda h: (h, 0, 0))
    square = pl.BlockSpec((1, rows, rows), lambda h: (h, 0, 0))
    state = pl.BlockSpec((1, width, width), lambda h: (h, 0, 0))
    state_list = pl.BlockSpec((1, spans, width, width), lambda h: (h, 0, 0, 0))
    inputs = [token] * 5 + [table]
    narrow_t = jax.ShapeDtypeStruct((heads, rows, width), F32)
    square_t = jax.ShapeDtypeStruct((heads, rows, rows), F32)
    state_t = jax.ShapeDtypeStruct((heads, width, width), F32)
    state_list_t = jax.ShapeDtypeStruct((heads, spans, width, width), F32)
    token_t = jax.ShapeDtypeStruct((rows, heads * width), BF16)
    params = pltpu.CompilerParams(dimension_semantics=("arbitrary",), vmem_limit_bytes=40 * 1024 * 1024)
    saved_specs = [narrow] * 2 + [square] * 3 + [state_list] * 3
    saved_types = [narrow_t] * 2 + [square_t] * 3 + [state_list_t] * 3
    results = pl.pallas_call(
        functools.partial(local_kernel, SPAN),
        grid=(heads,),
        in_specs=inputs,
        out_specs=saved_specs + [state] * 3,
        out_shape=saved_types + [state_t] * 3,
        compiler_params=params,
        name="local_part",
    )(q, k, v, g, o, s)
    saved = results[:8]
    ends, trans, inject = results[8:]
    state_in, grad_in = relay(trans, ends, inject)
    dq, dk, dv, dg, ds = pl.pallas_call(
        functools.partial(grad_kernel, SPAN),
        grid=(heads,),
        in_specs=inputs + saved_specs + [state] * 2,
        out_specs=[token] * 4 + [table],
        out_shape=[token_t] * 4 + [jax.ShapeDtypeStruct((rows, heads), F32)],
        compiler_params=params,
        name="grad_part",
    )(q, k, v, g, o, s, *saved, state_in, grad_in)

    def returned(array):
        return lax.all_to_all(array, "head", split_axis=0, concat_axis=1, tiled=True)

    return (returned(dq), returned(dk), returned(dv), returned(ds.astype(BF16)), returned(dg))


def solution(mesh):
    spec = P(("ctx", "head"), None)
    return jax.shard_map(
        per_device, mesh=mesh, in_specs=(spec,) * 6, out_specs=(spec,) * 5, check_vma=False
    )
```

```python
import functools

import jax
import jax.numpy as jnp
from jax import lax
from jax.experimental import pallas as pl
from jax.experimental.pallas import tpu as pltpu
from jax.sharding import PartitionSpec as P

SPAN = 64
BASE = 8
EPS = 1e-06
F32 = jnp.float32
BF16 = jnp.bfloat16
MESH = pl.DeviceIdType.MESH

NN = (((1,), (0,)), ((), ()))
NT = (((1,), (1,)), ((), ()))


def split(x):
    high = x.astype(BF16)
    return high, (x - high.astype(F32)).astype(BF16)


def mul(a, b, dims=NN):
    return lax.dot_general(a, b, dims, preferred_element_type=F32)


def dot3(a, b, dims=NN):
    if not isinstance(a, tuple):
        return mul(a, b[0], dims) + mul(a, b[1], dims)
    if not isinstance(b, tuple):
        return mul(a[0], b, dims) + mul(a[1], b, dims)
    return mul(a[0], b[0], dims) + (mul(a[0], b[1], dims) + mul(a[1], b[0], dims))


def rows_of(pair, start, size):
    if not isinstance(pair, tuple):
        return pair[start : start + size]
    return tuple(part[start : start + size] for part in pair)


def both(a, b, axis):
    return tuple(jnp.concatenate([x, y], axis=axis) for x, y in zip(a, b))


def grids(size):
    return (
        lax.broadcasted_iota(jnp.int32, (size, size), 0),
        lax.broadcasted_iota(jnp.int32, (size, size), 1),
    )


def per_span(row_values, span, like):
    rows, width = like.shape
    return jnp.broadcast_to(row_values, (rows // span, span, width)).reshape(rows, width)


def gates(g, span):
    rows, width = g.shape
    row, col = grids(rows)
    sum_mask = jnp.where((row // span == col // span) & (col <= row), 1.0, 0.0).astype(BF16)
    gamma = mul(sum_mask, g)
    spans = gamma.reshape(rows // span, span, width)
    middle = spans[:, span // 2 - 1 : span // 2]
    end = spans[:, span - 1 : span]
    centred = gamma - per_span(middle, span, gamma)
    rise = jnp.exp(centred)
    fall = jnp.exp(-centred)
    head = rise * per_span(jnp.exp(middle), span, gamma)
    tail = fall * per_span(jnp.exp(end - middle), span, gamma)
    fade = jnp.exp(end).reshape(rows // span, width)
    return rise, fall, head, tail, fade


def column_of(table, index):
    lane = lax.broadcasted_iota(jnp.int32, table.shape, 1)
    return jnp.sum(jnp.where(lane == index, table, 0.0), axis=1, keepdims=True)


def norm_of(x):
    return lax.rsqrt(jnp.sum(x * x, axis=1, keepdims=True) + EPS)


def inverse(system, row, col):
    same = row // BASE == col // BASE
    near = jnp.where(same, system, 0.0)
    near_s = split(near)
    square = dot3(near_s, near_s)
    square_s = split(square)
    found = jnp.where(row == col, 1.0, 0.0) - near
    fourth = dot3(square_s, square_s)
    found = found + dot3(split(found), square_s)
    found = found + dot3(split(found), split(fourth))
    block = BASE
    while block < SPAN:
        wide = row // (2 * block) == col // (2 * block)
        off = jnp.where(wide & (row // block != col // block), system, 0.0)
        found_s = split(found)
        found = found - dot3(found_s, split(dot3(split(off), found_s)))
        block *= 2
    return found


def local_kernel(span, q_ref, k_ref, v_ref, g_ref, o_ref, b_ref, ev_ref, ek_ref, inv_ref, a_ref, sc_ref,
                 tr_ref, bs_ref, gs_ref, end_ref, trans_ref, inject_ref):
    head_index = pl.program_id(0)
    rows, width = q_ref.shape
    spans = rows // span
    q = q_ref[...].astype(F32)
    k = k_ref[...].astype(F32)
    v = v_ref[...]
    o = o_ref[...]
    beta = column_of(b_ref[...], head_index)
    rise, fall, head, tail, fade = gates(g_ref[...], span)
    q_unit = q * norm_of(q) * width ** (-0.5)
    k_unit = k * norm_of(k)
    row, col = grids(rows)
    inside = row // span == col // span
    k_fall_s = split(k_unit * fall)
    inner = jnp.where(inside & (col < row), dot3(split(k_unit * rise), k_fall_s, NT), 0.0)
    scores = jnp.where(inside & (col <= row), dot3(split(q_unit * rise), k_fall_s, NT), 0.0)
    a_ref[0] = inner
    sc_ref[0] = scores
    beta_row = jnp.sum(jnp.where(row == col, beta, 0.0), axis=0, keepdims=True)
    found = inverse(inner * beta_row, row, col)
    inv_ref[0] = found
    found_s = split(found)
    e_value = dot3(found_s, v)
    e_key = dot3(found_s, split(k_unit * head))
    ev_ref[0] = e_value
    ek_ref[0] = e_key
    w_key_s = split(e_key * beta)
    w_value_s = split(e_value * beta)
    reach = q_unit * head - dot3(split(scores), w_key_s)
    k_tail = k_unit * tail
    small_row, small_col = grids(width)
    diagonal = small_row == small_col
    moves, adds, backs = [], [], []
    for index in range(spans):
        at = index * span
        tail_t = split(k_tail[at : at + span].T)
        move = jnp.where(diagonal, fade[index : index + 1], 0.0) - dot3(tail_t, rows_of(w_key_s, at, span))
        add = dot3(tail_t, rows_of(w_value_s, at, span))
        back = dot3(split(reach[at : at + span].T), o[at : at + span])
        tr_ref[0, index] = move
        bs_ref[0, index] = add
        gs_ref[0, index] = back
        moves.append(move)
        adds.append(add)
        backs.append(back)
    trans, ends = moves[0], adds[0]
    grad = backs[spans - 1]
    for index in range(1, spans):
        move_s = split(moves[index])
        trans = dot3(move_s, split(trans))
        ends = dot3(move_s, split(ends)) + adds[index]
        mirror = spans - 1 - index
        grad = dot3(split(moves[mirror].T), split(grad)) + backs[mirror]
    trans_ref[0] = trans
    end_ref[0] = ends
    inject_ref[0] = grad


def grad_kernel(span, q_ref, k_ref, v_ref, g_ref, o_ref, b_ref, ev_ref, ek_ref, inv_ref, a_ref, sc_ref,
                tr_ref, bs_ref, gs_ref, state_ref, dstate_ref, dq_ref, dk_ref, dv_ref, dg_ref, db_ref):
    head_index = pl.program_id(0)
    rows, width = q_ref.shape
    spans = rows // span
    q = q_ref[...].astype(F32)
    k = k_ref[...].astype(F32)
    o = o_ref[...]
    beta = column_of(b_ref[...], head_index)
    rise, fall, head, tail, fade = gates(g_ref[...], span)
    q_norm = norm_of(q)
    k_norm = norm_of(k)
    q_unit = q * q_norm * width ** (-0.5)
    k_unit = k * k_norm
    row, col = grids(rows)
    inside = row // span == col // span
    states = [state_ref[0]]
    grads = [dstate_ref[0]]
    for index in range(spans - 1):
        states.append(dot3(split(tr_ref[0, index]), split(states[-1])) + bs_ref[0, index])
        mirror = spans - 1 - index
        grads.insert(0, dot3(split(tr_ref[0, mirror].T), split(grads[0])) + gs_ref[0, mirror])
    states_s = [split(x) for x in states]
    grads_s = [split(x) for x in grads]

    def each(fn):
        return jnp.concatenate([fn(index, index * span) for index in range(spans)], axis=0)

    ek_s = split(ek_ref[0])
    k_tail = k_unit * tail
    k_tail_s = split(k_tail)
    error = ev_ref[0] - each(lambda i, at: dot3(rows_of(ek_s, at, span), states_s[i]))
    update_s = split(error * beta)
    d_update = dot3(split(sc_ref[0].T), o) + each(lambda i, at: dot3(rows_of(k_tail_s, at, span), grads_s[i]))
    d_value = dot3(split(inv_ref[0].T), split(d_update * beta))
    d_value_s = split(d_value)
    dv_ref[...] = d_value.astype(BF16)
    residue = d_update - dot3(split(a_ref[0].T), d_value_s)
    d_beta = jnp.sum(error * residue, axis=1, keepdims=True)
    lane = lax.broadcasted_iota(jnp.int32, b_ref.shape, 1)
    db_ref[...] = jnp.where(lane == head_index, d_beta, db_ref[...])
    dq_head = each(lambda i, at: dot3(o[at : at + span], states_s[i], NT))
    dk_head = -each(lambda i, at: dot3(rows_of(d_value_s, at, span), states_s[i], NT))
    dk_tail = each(lambda i, at: dot3(rows_of(update_s, at, span), grads_s[i], NT))
    d_scores = jnp.where(inside & (col <= row), dot3(o, update_s, NT), 0.0)
    d_inner = jnp.where(inside & (col < row), -dot3(d_value_s, update_s, NT), 0.0)
    k_fall_s = split(k_unit * fall)
    dq_rise = dot3(split(d_scores), k_fall_s)
    dk_rise = dot3(split(d_inner), k_fall_s)
    dk_fall = dot3(split(d_scores.T), split(q_unit * rise)) + dot3(split(d_inner.T), split(k_unit * rise))
    dq_unit = dq_rise * rise + dq_head * head
    up = dk_rise * rise + dk_head * head
    tail_part = dk_tail * tail
    down = dk_fall * fall + tail_part
    d_gamma = q_unit * dq_unit + k_unit * (up - down)
    tail_sum = jnp.sum((k_unit * tail_part).reshape(spans, span, width), axis=1, keepdims=True)
    small_row, small_col = grids(width)
    diagonal = small_row == small_col
    last = []
    for index in range(spans):
        d_fade = jnp.sum(states[index] * grads[index], axis=1, keepdims=True)
        d_fade = jnp.sum(jnp.where(diagonal, d_fade, 0.0), axis=0, keepdims=True)
        last.append(d_fade * fade[index : index + 1])
    last = jnp.concatenate([x.reshape(1, 1, width) for x in last], axis=0)
    sum_mask = jnp.where(inside & (col >= row), 1.0, 0.0).astype(BF16)
    d_decay = dot3(sum_mask, split(d_gamma)) + per_span(tail_sum + last, span, d_gamma)
    dg_ref[...] = d_decay.astype(BF16)
    scale = width ** (-0.5)
    dq = (dq_unit - q * (q_norm * q_norm * jnp.sum(q * dq_unit, axis=1, keepdims=True))) * (q_norm * scale)
    dq_ref[...] = dq.astype(BF16)
    dk_unit = up + down
    dk = (dk_unit - k * (k_norm * k_norm * jnp.sum(k * dk_unit, axis=1, keepdims=True))) * k_norm
    dk_ref[...] = dk.astype(BF16)


def relay_kernel(n, trans_ref, end_ref, inject_ref, state_ref, grad_ref, move_ref, turn_ref, in_f, in_b, out_f, out_b,
                 recv_f, recv_b, send_f, send_b):
    me = lax.axis_index("ctx")
    heads = trans_ref.shape[0]
    first, last = me == 0, me == n - 1
    barrier = pltpu.get_barrier_semaphore()

    def push(out, arrive, send, recv, h, target):
        return pltpu.make_async_remote_copy(
            src_ref=out.at[h], dst_ref=arrive.at[h], send_sem=send.at[h], recv_sem=recv.at[h],
            device_id={"ctx": target}, device_id_type=MESH,
        )

    @pl.when(jnp.logical_not(first))
    def _():
        pl.semaphore_signal(barrier, inc=1, device_id={"ctx": me - 1}, device_id_type=MESH)

    @pl.when(jnp.logical_not(last))
    def _():
        pl.semaphore_signal(barrier, inc=1, device_id={"ctx": me + 1}, device_id_type=MESH)

    @pl.when(first)
    def _():
        in_f[...] = jnp.zeros_like(in_f)

    @pl.when(last)
    def _():
        in_b[...] = jnp.zeros_like(in_b)

    for h in range(heads):
        trans = trans_ref[h]
        move_ref[0, h], move_ref[1, h] = split(trans)
        turn_ref[0, h], turn_ref[1, h] = split(trans.T)

    @pl.when(first | last)
    def _():
        pl.semaphore_wait(barrier, 1)

    @pl.when(jnp.logical_not(first | last))
    def _():
        pl.semaphore_wait(barrier, 2)

    def forward(h):
        @pl.when(jnp.logical_not(first))
        def _():
            push(out_f, in_f, send_f, recv_f, h, me - 1).wait_recv()

        state = in_f[h]
        state_ref[h] = state

        @pl.when(jnp.logical_not(last))
        def _():
            out_f[h] = dot3((move_ref[0, h], move_ref[1, h]), split(state)) + end_ref[h]
            push(out_f, in_f, send_f, recv_f, h, me + 1).start()

    def backward(h):
        @pl.when(jnp.logical_not(last))
        def _():
            push(out_b, in_b, send_b, recv_b, h, me + 1).wait_recv()

        grad = in_b[h]
        grad_ref[h] = grad

        @pl.when(jnp.logical_not(first))
        def _():
            out_b[h] = dot3((turn_ref[0, h], turn_ref[1, h]), split(grad)) + inject_ref[h]
            push(out_b, in_b, send_b, recv_b, h, me - 1).start()

    early = 2 * me < n
    middle = (2 * me == n - 2) | (2 * me == n)
    lag = jnp.where(middle, min(3, heads), heads)
    lag_f = jnp.where(early, 0, lag)
    lag_b = jnp.where(early, lag, 0)

    def step(t, carry):
        @pl.when((t >= lag_f) & (t < lag_f + heads))
        def _():
            forward(t - lag_f)

        @pl.when((t >= lag_b) & (t < lag_b + heads))
        def _():
            backward(t - lag_b)

        return carry

    lax.fori_loop(0, 2 * heads, step, 0)

    def finish(h, carry):
        @pl.when(jnp.logical_not(last))
        def _():
            push(out_f, in_f, send_f, recv_f, h, me + 1).wait_send()

        @pl.when(jnp.logical_not(first))
        def _():
            push(out_b, in_b, send_b, recv_b, h, me - 1).wait_send()

        return carry

    lax.fori_loop(0, heads, finish, 0)


def relay(trans, ends, inject):
    heads, width = trans.shape[:2]
    whole = pl.BlockSpec(memory_space=pltpu.VMEM)
    state_t = jax.ShapeDtypeStruct((heads, width, width), F32)
    held = pltpu.VMEM((heads, width, width), F32)
    halves = pltpu.VMEM((2, heads, width, width), BF16)
    return pl.pallas_call(
        functools.partial(relay_kernel, lax.axis_size("ctx")),
        in_specs=[whole] * 3,
        out_specs=[whole] * 2,
        out_shape=[state_t] * 2,
        scratch_shapes=[halves] * 2 + [held] * 4 + [pltpu.SemaphoreType.DMA((heads,))] * 4,
        compiler_params=pltpu.CompilerParams(
            collective_id=0, has_side_effects=True, vmem_limit_bytes=40 * 1024 * 1024
        ),
        name="relay",
    )(trans, ends, inject)


def exchange_kernel(n, count, source, target, *refs):
    ins, outs = refs[:count], refs[count : 2 * count]
    send, recv, own = refs[2 * count :]
    me = lax.axis_index("head")
    barrier = pltpu.get_barrier_semaphore()
    for step in range(1, n):
        pl.semaphore_signal(
            barrier, inc=1, device_id={"head": lax.rem(me + step, n)}, device_id_type=MESH
        )
    local = [
        pltpu.make_async_copy(source(i, a, me), target(i, b, me), own.at[i])
        for i, (a, b) in enumerate(zip(ins, outs))
    ]
    for copy in local:
        copy.start()
    pl.semaphore_wait(barrier, n - 1)
    copies = []
    for i, (a, b) in enumerate(zip(ins, outs)):
        for step in range(1, n):
            peer = lax.rem(me + step, n)
            copy = pltpu.make_async_remote_copy(
                src_ref=source(i, a, peer), dst_ref=target(i, b, me), send_sem=send.at[i, step],
                recv_sem=recv.at[i, step], device_id={"head": peer}, device_id_type=MESH,
            )
            copy.start()
            copies.append(copy)
    for copy in local + copies:
        copy.wait()


def exchange(arrays, types, source, target, identity, name):
    count, n = len(arrays), lax.axis_size("head")
    whole = pl.BlockSpec(memory_space=pltpu.VMEM)
    return pl.pallas_call(
        functools.partial(exchange_kernel, n, count, source, target),
        in_specs=[whole] * count,
        out_specs=[whole] * count,
        out_shape=types,
        scratch_shapes=[pltpu.SemaphoreType.DMA((count, n))] * 2 + [pltpu.SemaphoreType.DMA((count,))],
        compiler_params=pltpu.CompilerParams(
            collective_id=identity, has_side_effects=True, vmem_limit_bytes=40 * 1024 * 1024
        ),
        name=name,
    )(*arrays)


def per_device(queries, key_in, values_in, strength, log_decay, d_out):
    heads_all = strength.shape[1]
    heads = heads_all // lax.axis_size("head")
    width = queries.shape[1] // heads_all

    n = lax.axis_size("head")
    share = queries.shape[0]
    local_width = heads * width

    def columns(index, ref, peer):
        if index == 5:
            return ref
        return ref.at[:, pl.ds(pl.multiple_of(peer * local_width, local_width), local_width)]

    def tokens(index, ref, peer):
        return ref.at[pl.ds(pl.multiple_of(peer * share, share), share)]

    k, g, q, v, o, s = exchange(
        (key_in, log_decay, queries, values_in, d_out, strength),
        [jax.ShapeDtypeStruct((n * share, local_width), BF16)] * 5
        + [jax.ShapeDtypeStruct((n * share, heads_all), BF16)],
        columns, tokens, 1, "gather_heads",
    )
    s = lax.dynamic_slice_in_dim(s, lax.axis_index("head") * heads, heads, axis=1)
    s = s.astype(F32)
    rows = q.shape[0]
    spans = rows // SPAN
    token = pl.BlockSpec((rows, width), lambda h: (0, h))
    table = pl.BlockSpec((rows, heads), lambda h: (0, 0))
    narrow = pl.BlockSpec((1, rows, width), lambda h: (h, 0, 0))
    square = pl.BlockSpec((1, rows, rows), lambda h: (h, 0, 0))
    state = pl.BlockSpec((1, width, width), lambda h: (h, 0, 0))
    state_list = pl.BlockSpec((1, spans, width, width), lambda h: (h, 0, 0, 0))
    inputs = [token] * 5 + [table]
    narrow_t = jax.ShapeDtypeStruct((heads, rows, width), F32)
    square_t = jax.ShapeDtypeStruct((heads, rows, rows), F32)
    state_t = jax.ShapeDtypeStruct((heads, width, width), F32)
    state_list_t = jax.ShapeDtypeStruct((heads, spans, width, width), F32)
    token_t = jax.ShapeDtypeStruct((rows, heads * width), BF16)
    params = pltpu.CompilerParams(dimension_semantics=("arbitrary",), vmem_limit_bytes=40 * 1024 * 1024)
    saved_specs = [narrow] * 2 + [square] * 3 + [state_list] * 3
    saved_types = [narrow_t] * 2 + [square_t] * 3 + [state_list_t] * 3
    results = pl.pallas_call(
        functools.partial(local_kernel, SPAN),
        grid=(heads,),
        in_specs=inputs,
        out_specs=saved_specs + [state] * 3,
        out_shape=saved_types + [state_t] * 3,
        compiler_params=params,
        name="local_part",
    )(q, k, v, g, o, s)
    saved = results[:8]
    ends, trans, inject = results[8:]
    state_in, grad_in = relay(trans, ends, inject)
    dq, dk, dv, dg, ds = pl.pallas_call(
        functools.partial(grad_kernel, SPAN),
        grid=(heads,),
        in_specs=inputs + saved_specs + [state] * 2,
        out_specs=[token] * 4 + [table],
        out_shape=[token_t] * 4 + [jax.ShapeDtypeStruct((rows, heads), F32)],
        compiler_params=params,
        name="grad_part",
    )(q, k, v, g, o, s, *saved, state_in, grad_in)

    def own_columns(index, ref, peer):
        return ref.at[peer] if index == 4 else columns(index, ref, peer)

    dq, dk, dv, dg, ds = exchange(
        (dq, dk, dv, dg, ds.astype(BF16)),
        [jax.ShapeDtypeStruct((share, n * local_width), BF16)] * 4
        + [jax.ShapeDtypeStruct((n, share, heads), BF16)],
        tokens, own_columns, 2, "return_heads",
    )
    return dq, dk, dv, jnp.transpose(ds, (1, 0, 2)).reshape(share, heads_all), dg


def solution(mesh):
    spec = P(("ctx", "head"), None)
    return jax.shard_map(
        per_device, mesh=mesh, in_specs=(spec,) * 6, out_specs=(spec,) * 5, check_vma=False
    )
```

```python
import functools

import jax
import jax.numpy as jnp
from jax import lax
from jax.experimental import pallas as pl
from jax.experimental.pallas import tpu as pltpu
from jax.sharding import PartitionSpec as P

SPAN = 64
BASE = 8
EPS = 1e-06
F32 = jnp.float32
BF16 = jnp.bfloat16
MESH = pl.DeviceIdType.MESH

NN = (((1,), (0,)), ((), ()))
NT = (((1,), (1,)), ((), ()))


def split(x):
    high = x.astype(BF16)
    return high, (x - high.astype(F32)).astype(BF16)


def mul(a, b, dims=NN):
    return lax.dot_general(a, b, dims, preferred_element_type=F32)


def dot3(a, b, dims=NN):
    if not isinstance(a, tuple):
        return mul(a, b[0], dims) + mul(a, b[1], dims)
    if not isinstance(b, tuple):
        return mul(a[0], b, dims) + mul(a[1], b, dims)
    return mul(a[0], b[0], dims) + (mul(a[0], b[1], dims) + mul(a[1], b[0], dims))


def rows_of(pair, start, size):
    if not isinstance(pair, tuple):
        return pair[start : start + size]
    return tuple(part[start : start + size] for part in pair)


def both(a, b, axis):
    return tuple(jnp.concatenate([x, y], axis=axis) for x, y in zip(a, b))


def grids(size):
    return (
        lax.broadcasted_iota(jnp.int32, (size, size), 0),
        lax.broadcasted_iota(jnp.int32, (size, size), 1),
    )


def per_span(row_values, span, like):
    rows, width = like.shape
    return jnp.broadcast_to(row_values, (rows // span, span, width)).reshape(rows, width)


def gates(g, span):
    rows, width = g.shape
    row, col = grids(rows)
    sum_mask = jnp.where((row // span == col // span) & (col <= row), 1.0, 0.0).astype(BF16)
    gamma = mul(sum_mask, g)
    spans = gamma.reshape(rows // span, span, width)
    middle = spans[:, span // 2 - 1 : span // 2]
    end = spans[:, span - 1 : span]
    centred = gamma - per_span(middle, span, gamma)
    rise = jnp.exp(centred)
    fall = jnp.exp(-centred)
    head = rise * per_span(jnp.exp(middle), span, gamma)
    tail = fall * per_span(jnp.exp(end - middle), span, gamma)
    fade = jnp.exp(end).reshape(rows // span, width)
    return rise, fall, head, tail, fade


def column_of(table, index):
    lane = lax.broadcasted_iota(jnp.int32, table.shape, 1)
    return jnp.sum(jnp.where(lane == index, table, 0.0), axis=1, keepdims=True)


def norm_of(x):
    return lax.rsqrt(jnp.sum(x * x, axis=1, keepdims=True) + EPS)


def inverse(system, row, col):
    same = row // BASE == col // BASE
    near = jnp.where(same, system, 0.0)
    near_s = split(near)
    square = dot3(near_s, near_s)
    square_s = split(square)
    found = jnp.where(row == col, 1.0, 0.0) - near
    fourth = dot3(square_s, square_s)
    found = found + dot3(split(found), square_s)
    found = found + dot3(split(found), split(fourth))
    block = BASE
    while block < SPAN:
        wide = row // (2 * block) == col // (2 * block)
        off = jnp.where(wide & (row // block != col // block), system, 0.0)
        found_s = split(found)
        found = found - dot3(found_s, split(dot3(split(off), found_s)))
        block *= 2
    return found


def gather_head(n, ins, held, table_ref, table_held, send, recv, own, t_send, t_recv, t_own):
    me = lax.axis_index("head")
    step_index = pl.program_id(0)
    heads, rows, width = held.shape[1:]
    share = rows // n
    mine = pl.ds(pl.multiple_of(me * share, share), share)

    def source(index, h, peer):
        return ins[index].at[:, pl.ds(pl.multiple_of((peer * heads + h) * width, width), width)]

    def local(index, h):
        return pltpu.make_async_copy(source(index, h, me), held.at[index, h, mine], own.at[h, index])

    def remote(index, h, step):
        peer = lax.rem(me + step, n)
        return pltpu.make_async_remote_copy(
            src_ref=source(index, h, peer), dst_ref=held.at[index, h, mine], send_sem=send.at[h, index, step],
            recv_sem=recv.at[h, index, step], device_id={"head": peer}, device_id_type=MESH,
        )

    def table_local():
        return pltpu.make_async_copy(table_ref, table_held.at[mine], t_own)

    def table_remote(step):
        return pltpu.make_async_remote_copy(
            src_ref=table_ref, dst_ref=table_held.at[mine], send_sem=t_send.at[step],
            recv_sem=t_recv.at[step], device_id={"head": lax.rem(me + step, n)}, device_id_type=MESH,
        )

    @pl.when(step_index == 0)
    def _():
        barrier = pltpu.get_barrier_semaphore()
        for step in range(1, n):
            pl.semaphore_signal(
                barrier, inc=1, device_id={"head": lax.rem(me + step, n)}, device_id_type=MESH
            )
        table_local().start()

        def start_local(h, carry):
            for index in range(len(ins)):
                local(index, h).start()
            return carry

        lax.fori_loop(0, heads, start_local, 0)
        pl.semaphore_wait(barrier, n - 1)
        for step in range(1, n):
            table_remote(step).start()

        def start_remote(h, carry):
            for index in range(len(ins)):
                for step in range(1, n):
                    remote(index, h, step).start()
            return carry

        lax.fori_loop(0, heads, start_remote, 0)
        table_local().wait()
        for step in range(1, n):
            table_remote(step).wait_recv()

    for index in range(len(ins)):
        local(index, step_index).wait()
        for step in range(1, n):
            remote(index, step_index, step).wait_recv()

    @pl.when(step_index == heads - 1)
    def _():
        for step in range(1, n):
            table_remote(step).wait_send()

        def finish(h, carry):
            for index in range(len(ins)):
                for step in range(1, n):
                    remote(index, h, step).wait_send()
            return carry

        lax.fori_loop(0, heads, finish, 0)


def local_kernel(n, span, q_ref, k_ref, v_ref, g_ref, o_ref, b_ref, ev_ref, ek_ref, inv_ref, a_ref, sc_ref,
                 tr_ref, bs_ref, gs_ref, end_ref, trans_ref, inject_ref, q_out, k_out, g_out, o_out, beta_out,
                 held, table_held, send, recv, own, t_send, t_recv, t_own):
    head_index = pl.program_id(0)
    gather_head(n, (k_ref, g_ref, q_ref, v_ref, o_ref), held, b_ref, table_held, send, recv, own, t_send, t_recv, t_own)
    heads, rows, width = held.shape[1:]
    spans = rows // span
    k_raw, g, q_raw, v, o = (held[index, head_index] for index in range(5))
    k_out[0], g_out[0], q_out[0], o_out[0] = k_raw, g, q_raw, o
    q = q_raw.astype(F32)
    k = k_raw.astype(F32)
    beta = column_of(table_held[...].astype(F32), lax.axis_index("head") * heads + head_index)
    beta_out[0] = beta
    rise, fall, head, tail, fade = gates(g, span)
    q_unit = q * norm_of(q) * width ** (-0.5)
    k_unit = k * norm_of(k)
    row, col = grids(rows)
    inside = row // span == col // span
    k_fall_s = split(k_unit * fall)
    inner = jnp.where(inside & (col < row), dot3(split(k_unit * rise), k_fall_s, NT), 0.0)
    scores = jnp.where(inside & (col <= row), dot3(split(q_unit * rise), k_fall_s, NT), 0.0)
    a_ref[0] = inner
    sc_ref[0] = scores
    beta_row = jnp.sum(jnp.where(row == col, beta, 0.0), axis=0, keepdims=True)
    found = inverse(inner * beta_row, row, col)
    inv_ref[0] = found
    found_s = split(found)
    e_value = dot3(found_s, v)
    e_key = dot3(found_s, split(k_unit * head))
    ev_ref[0] = e_value
    ek_ref[0] = e_key
    w_key_s = split(e_key * beta)
    w_value_s = split(e_value * beta)
    reach = q_unit * head - dot3(split(scores), w_key_s)
    k_tail = k_unit * tail
    small_row, small_col = grids(width)
    diagonal = small_row == small_col
    moves, adds, backs = [], [], []
    for index in range(spans):
        at = index * span
        tail_t = split(k_tail[at : at + span].T)
        move = jnp.where(diagonal, fade[index : index + 1], 0.0) - dot3(tail_t, rows_of(w_key_s, at, span))
        add = dot3(tail_t, rows_of(w_value_s, at, span))
        back = dot3(split(reach[at : at + span].T), o[at : at + span])
        tr_ref[0, index] = move
        bs_ref[0, index] = add
        gs_ref[0, index] = back
        moves.append(move)
        adds.append(add)
        backs.append(back)
    trans, ends = moves[0], adds[0]
    grad = backs[spans - 1]
    for index in range(1, spans):
        move_s = split(moves[index])
        trans = dot3(move_s, split(trans))
        ends = dot3(move_s, split(ends)) + adds[index]
        mirror = spans - 1 - index
        grad = dot3(split(moves[mirror].T), split(grad)) + backs[mirror]
    trans_ref[0] = trans
    end_ref[0] = ends
    inject_ref[0] = grad


def grad_kernel(n, span, q_ref, k_ref, g_ref, o_ref, b_ref, ev_ref, ek_ref, inv_ref, a_ref, sc_ref,
                tr_ref, bs_ref, gs_ref, state_ref, dstate_ref, dq_out, dk_out, dv_out, dg_out, db_out,
                done, db_all, db_done, send, recv, own, t_send, t_recv, t_own):
    head_index = pl.program_id(0)
    me = lax.axis_index("head")
    outs = (dv_out, dq_out, dk_out, dg_out)
    heads, rows, width = done.shape[1:]
    share = rows // n
    spans = rows // span

    def part(peer):
        return pl.ds(pl.multiple_of(peer * share, share), share)

    def target(index, h):
        return outs[index].at[:, pl.ds(pl.multiple_of((me * heads + h) * width, width), width)]

    def local(index, h):
        return pltpu.make_async_copy(done.at[index, h, part(me)], target(index, h), own.at[h, index])

    def remote(index, h, step):
        peer = lax.rem(me + step, n)
        return pltpu.make_async_remote_copy(
            src_ref=done.at[index, h, part(peer)], dst_ref=target(index, h), send_sem=send.at[h, index, step],
            recv_sem=recv.at[h, index, step], device_id={"head": peer}, device_id_type=MESH,
        )

    def table_local():
        return pltpu.make_async_copy(db_done.at[part(me)], db_out.at[me], t_own)

    def table_remote(step):
        peer = lax.rem(me + step, n)
        return pltpu.make_async_remote_copy(
            src_ref=db_done.at[part(peer)], dst_ref=db_out.at[me], send_sem=t_send.at[step],
            recv_sem=t_recv.at[step], device_id={"head": peer}, device_id_type=MESH,
        )

    def emit(index, value):
        done[index, head_index] = value.astype(BF16)
        local(index, head_index).start()
        for step in range(1, n):
            remote(index, head_index, step).start()

    @pl.when(head_index == 0)
    def _():
        barrier = pltpu.get_barrier_semaphore()
        for step in range(1, n):
            pl.semaphore_signal(
                barrier, inc=1, device_id={"head": lax.rem(me + step, n)}, device_id_type=MESH
            )
        db_all[...] = jnp.zeros_like(db_all)
        pl.semaphore_wait(barrier, n - 1)

    q = q_ref[0].astype(F32)
    k = k_ref[0].astype(F32)
    o = o_ref[0]
    beta = b_ref[0]
    rise, fall, head, tail, fade = gates(g_ref[0], span)
    q_norm = norm_of(q)
    k_norm = norm_of(k)
    q_unit = q * q_norm * width ** (-0.5)
    k_unit = k * k_norm
    row, col = grids(rows)
    inside = row // span == col // span
    states = [state_ref[0]]
    grads = [dstate_ref[0]]
    for index in range(spans - 1):
        states.append(dot3(split(tr_ref[0, index]), split(states[-1])) + bs_ref[0, index])
        mirror = spans - 1 - index
        grads.insert(0, dot3(split(tr_ref[0, mirror].T), split(grads[0])) + gs_ref[0, mirror])
    states_s = [split(x) for x in states]
    grads_s = [split(x) for x in grads]

    def each(fn):
        return jnp.concatenate([fn(index, index * span) for index in range(spans)], axis=0)

    ek_s = split(ek_ref[0])
    k_tail = k_unit * tail
    k_tail_s = split(k_tail)
    error = ev_ref[0] - each(lambda i, at: dot3(rows_of(ek_s, at, span), states_s[i]))
    update_s = split(error * beta)
    d_update = dot3(split(sc_ref[0].T), o) + each(lambda i, at: dot3(rows_of(k_tail_s, at, span), grads_s[i]))
    d_value = dot3(split(inv_ref[0].T), split(d_update * beta))
    d_value_s = split(d_value)
    emit(0, d_value)
    residue = d_update - dot3(split(a_ref[0].T), d_value_s)
    d_beta = jnp.sum(error * residue, axis=1, keepdims=True)
    lane = lax.broadcasted_iota(jnp.int32, db_all.shape, 1)
    db_all[...] = jnp.where(lane == head_index, d_beta, db_all[...])
    dq_head = each(lambda i, at: dot3(o[at : at + span], states_s[i], NT))
    dk_head = -each(lambda i, at: dot3(rows_of(d_value_s, at, span), states_s[i], NT))
    dk_tail = each(lambda i, at: dot3(rows_of(update_s, at, span), grads_s[i], NT))
    d_scores = jnp.where(inside & (col <= row), dot3(o, update_s, NT), 0.0)
    d_inner = jnp.where(inside & (col < row), -dot3(d_value_s, update_s, NT), 0.0)
    k_fall_s = split(k_unit * fall)
    dq_rise = dot3(split(d_scores), k_fall_s)
    dk_rise = dot3(split(d_inner), k_fall_s)
    dk_fall = dot3(split(d_scores.T), split(q_unit * rise)) + dot3(split(d_inner.T), split(k_unit * rise))
    dq_unit = dq_rise * rise + dq_head * head
    up = dk_rise * rise + dk_head * head
    tail_part = dk_tail * tail
    down = dk_fall * fall + tail_part
    d_gamma = q_unit * dq_unit + k_unit * (up - down)
    tail_sum = jnp.sum((k_unit * tail_part).reshape(spans, span, width), axis=1, keepdims=True)
    small_row, small_col = grids(width)
    diagonal = small_row == small_col
    last = []
    for index in range(spans):
        d_fade = jnp.sum(states[index] * grads[index], axis=1, keepdims=True)
        d_fade = jnp.sum(jnp.where(diagonal, d_fade, 0.0), axis=0, keepdims=True)
        last.append(d_fade * fade[index : index + 1])
    last = jnp.concatenate([x.reshape(1, 1, width) for x in last], axis=0)
    sum_mask = jnp.where(inside & (col >= row), 1.0, 0.0).astype(BF16)
    d_decay = dot3(sum_mask, split(d_gamma)) + per_span(tail_sum + last, span, d_gamma)
    scale = width ** (-0.5)
    dq = (dq_unit - q * (q_norm * q_norm * jnp.sum(q * dq_unit, axis=1, keepdims=True))) * (q_norm * scale)
    emit(1, dq)
    dk_unit = up + down
    dk = (dk_unit - k * (k_norm * k_norm * jnp.sum(k * dk_unit, axis=1, keepdims=True))) * k_norm
    emit(2, dk)
    emit(3, d_decay)

    @pl.when(head_index == heads - 1)
    def _():
        db_done[...] = db_all[...].astype(BF16)
        table_local().start()
        for step in range(1, n):
            table_remote(step).start()

        def finish(h, carry):
            for index in range(len(outs)):
                local(index, h).wait()
                for step in range(1, n):
                    remote(index, h, step).wait()
            return carry

        lax.fori_loop(0, heads, finish, 0)
        table_local().wait()
        for step in range(1, n):
            table_remote(step).wait()


def relay_kernel(n, trans_ref, end_ref, inject_ref, state_ref, grad_ref, move_ref, turn_ref, in_f, in_b, out_f, out_b,
                 recv_f, recv_b, send_f, send_b):
    me = lax.axis_index("ctx")
    heads = trans_ref.shape[0]
    first, last = me == 0, me == n - 1
    barrier = pltpu.get_barrier_semaphore()

    def push(out, arrive, send, recv, h, target):
        return pltpu.make_async_remote_copy(
            src_ref=out.at[h], dst_ref=arrive.at[h], send_sem=send.at[h], recv_sem=recv.at[h],
            device_id={"ctx": target}, device_id_type=MESH,
        )

    @pl.when(jnp.logical_not(first))
    def _():
        pl.semaphore_signal(barrier, inc=1, device_id={"ctx": me - 1}, device_id_type=MESH)

    @pl.when(jnp.logical_not(last))
    def _():
        pl.semaphore_signal(barrier, inc=1, device_id={"ctx": me + 1}, device_id_type=MESH)

    @pl.when(first)
    def _():
        in_f[...] = jnp.zeros_like(in_f)

    @pl.when(last)
    def _():
        in_b[...] = jnp.zeros_like(in_b)

    for h in range(heads):
        trans = trans_ref[h]
        move_ref[0, h], move_ref[1, h] = split(trans)
        turn_ref[0, h], turn_ref[1, h] = split(trans.T)

    @pl.when(first | last)
    def _():
        pl.semaphore_wait(barrier, 1)

    @pl.when(jnp.logical_not(first | last))
    def _():
        pl.semaphore_wait(barrier, 2)

    def forward(h):
        @pl.when(jnp.logical_not(first))
        def _():
            push(out_f, in_f, send_f, recv_f, h, me - 1).wait_recv()

        state = in_f[h]
        state_ref[h] = state

        @pl.when(jnp.logical_not(last))
        def _():
            out_f[h] = dot3((move_ref[0, h], move_ref[1, h]), split(state)) + end_ref[h]
            push(out_f, in_f, send_f, recv_f, h, me + 1).start()

    def backward(h):
        @pl.when(jnp.logical_not(last))
        def _():
            push(out_b, in_b, send_b, recv_b, h, me + 1).wait_recv()

        grad = in_b[h]
        grad_ref[h] = grad

        @pl.when(jnp.logical_not(first))
        def _():
            out_b[h] = dot3((turn_ref[0, h], turn_ref[1, h]), split(grad)) + inject_ref[h]
            push(out_b, in_b, send_b, recv_b, h, me - 1).start()

    early = 2 * me < n
    middle = (2 * me == n - 2) | (2 * me == n)
    lag = jnp.where(middle, min(3, heads), heads)
    lag_f = jnp.where(early, 0, lag)
    lag_b = jnp.where(early, lag, 0)

    def step(t, carry):
        @pl.when((t >= lag_f) & (t < lag_f + heads))
        def _():
            forward(t - lag_f)

        @pl.when((t >= lag_b) & (t < lag_b + heads))
        def _():
            backward(t - lag_b)

        return carry

    lax.fori_loop(0, 2 * heads, step, 0)

    def finish(h, carry):
        @pl.when(jnp.logical_not(last))
        def _():
            push(out_f, in_f, send_f, recv_f, h, me + 1).wait_send()

        @pl.when(jnp.logical_not(first))
        def _():
            push(out_b, in_b, send_b, recv_b, h, me - 1).wait_send()

        return carry

    lax.fori_loop(0, heads, finish, 0)


def relay(trans, ends, inject):
    heads, width = trans.shape[:2]
    whole = pl.BlockSpec(memory_space=pltpu.VMEM)
    state_t = jax.ShapeDtypeStruct((heads, width, width), F32)
    held = pltpu.VMEM((heads, width, width), F32)
    halves = pltpu.VMEM((2, heads, width, width), BF16)
    return pl.pallas_call(
        functools.partial(relay_kernel, lax.axis_size("ctx")),
        in_specs=[whole] * 3,
        out_specs=[whole] * 2,
        out_shape=[state_t] * 2,
        scratch_shapes=[halves] * 2 + [held] * 4 + [pltpu.SemaphoreType.DMA((heads,))] * 4,
        compiler_params=pltpu.CompilerParams(
            collective_id=0, has_side_effects=True, vmem_limit_bytes=40 * 1024 * 1024
        ),
        name="relay",
    )(trans, ends, inject)


def per_device(queries, key_in, values_in, strength, log_decay, d_out):
    heads_all = strength.shape[1]
    n = lax.axis_size("head")
    heads = heads_all // n
    width = queries.shape[1] // heads_all
    share = queries.shape[0]
    rows = n * share
    spans = rows // SPAN
    outside = pl.BlockSpec(memory_space=pl.ANY)
    narrow = pl.BlockSpec((1, rows, width), lambda h: (h, 0, 0))
    square = pl.BlockSpec((1, rows, rows), lambda h: (h, 0, 0))
    state = pl.BlockSpec((1, width, width), lambda h: (h, 0, 0))
    state_list = pl.BlockSpec((1, spans, width, width), lambda h: (h, 0, 0, 0))
    column = pl.BlockSpec((1, rows, 1), lambda h: (h, 0, 0))
    narrow_t = jax.ShapeDtypeStruct((heads, rows, width), F32)
    token_t = jax.ShapeDtypeStruct((heads, rows, width), BF16)
    square_t = jax.ShapeDtypeStruct((heads, rows, rows), F32)
    state_t = jax.ShapeDtypeStruct((heads, width, width), F32)
    state_list_t = jax.ShapeDtypeStruct((heads, spans, width, width), F32)
    column_t = jax.ShapeDtypeStruct((heads, rows, 1), F32)
    dma = pltpu.SemaphoreType.DMA

    def params(identity):
        return pltpu.CompilerParams(
            dimension_semantics=("arbitrary",), vmem_limit_bytes=48 * 1024 * 1024,
            collective_id=identity, has_side_effects=True,
        )

    def semaphores(count):
        return [dma((heads, count, n))] * 2 + [dma((heads, count))] + [dma((n,))] * 2 + [dma(())]

    saved_specs = [narrow] * 2 + [square] * 3 + [state_list] * 3
    saved_types = [narrow_t] * 2 + [square_t] * 3 + [state_list_t] * 3
    results = pl.pallas_call(
        functools.partial(local_kernel, n, SPAN),
        grid=(heads,),
        in_specs=[outside] * 6,
        out_specs=saved_specs + [state] * 3 + [narrow] * 4 + [column],
        out_shape=saved_types + [state_t] * 3 + [token_t] * 4 + [column_t],
        scratch_shapes=[pltpu.VMEM((5, heads, rows, width), BF16), pltpu.VMEM((rows, heads_all), BF16)] + semaphores(5),
        compiler_params=params(1),
        name="local_part",
    )(queries, key_in, values_in, log_decay, d_out, strength)
    saved = results[:8]
    ends, trans, inject = results[8:11]
    moved = results[11:]
    state_in, grad_in = relay(trans, ends, inject)
    full_t = jax.ShapeDtypeStruct(queries.shape, BF16)
    dq, dk, dv, dg, ds = pl.pallas_call(
        functools.partial(grad_kernel, n, SPAN),
        grid=(heads,),
        in_specs=[narrow] * 4 + [column] + saved_specs + [state] * 2,
        out_specs=[outside] * 5,
        out_shape=[full_t] * 4 + [jax.ShapeDtypeStruct((n, share, heads), BF16)],
        scratch_shapes=[
            pltpu.VMEM((4, heads, rows, width), BF16), pltpu.VMEM((rows, heads), F32), pltpu.VMEM((rows, heads), BF16)
        ] + semaphores(4),
        compiler_params=params(2),
        name="grad_part",
    )(*moved, *saved, state_in, grad_in)
    return dq, dk, dv, jnp.transpose(ds, (1, 0, 2)).reshape(share, heads_all), dg


def solution(mesh):
    spec = P(("ctx", "head"), None)
    return jax.shard_map(
        per_device, mesh=mesh, in_specs=(spec,) * 6, out_specs=(spec,) * 5, check_vma=False
    )
```

```python
import functools

import jax
import jax.numpy as jnp
from jax import lax
from jax.experimental import pallas as pl
from jax.experimental.pallas import tpu as pltpu
from jax.sharding import PartitionSpec as P

SPAN = 64
BASE = 8
EPS = 1e-06
F32 = jnp.float32
BF16 = jnp.bfloat16
MESH = pl.DeviceIdType.MESH

NN = (((1,), (0,)), ((), ()))
NT = (((1,), (1,)), ((), ()))


def split(x):
    high = x.astype(BF16)
    return high, (x - high.astype(F32)).astype(BF16)


def mul(a, b, dims=NN):
    return lax.dot_general(a, b, dims, preferred_element_type=F32)


def dot3(a, b, dims=NN):
    if not isinstance(a, tuple):
        return mul(a, b[0], dims) + mul(a, b[1], dims)
    if not isinstance(b, tuple):
        return mul(a[0], b, dims) + mul(a[1], b, dims)
    return mul(a[0], b[0], dims) + (mul(a[0], b[1], dims) + mul(a[1], b[0], dims))


def rows_of(pair, start, size):
    if not isinstance(pair, tuple):
        return pair[start : start + size]
    return tuple(part[start : start + size] for part in pair)


def both(a, b, axis):
    return tuple(jnp.concatenate([x, y], axis=axis) for x, y in zip(a, b))


def grids(size):
    return (
        lax.broadcasted_iota(jnp.int32, (size, size), 0),
        lax.broadcasted_iota(jnp.int32, (size, size), 1),
    )


def per_span(row_values, span, like):
    rows, width = like.shape
    return jnp.broadcast_to(row_values, (rows // span, span, width)).reshape(rows, width)


def gates(g, span):
    rows, width = g.shape
    row, col = grids(rows)
    sum_mask = jnp.where((row // span == col // span) & (col <= row), 1.0, 0.0).astype(BF16)
    gamma = mul(sum_mask, g)
    spans = gamma.reshape(rows // span, span, width)
    middle = spans[:, span // 2 - 1 : span // 2]
    end = spans[:, span - 1 : span]
    centred = gamma - per_span(middle, span, gamma)
    rise = jnp.exp(centred)
    fall = jnp.exp(-centred)
    head = rise * per_span(jnp.exp(middle), span, gamma)
    tail = fall * per_span(jnp.exp(end - middle), span, gamma)
    fade = jnp.exp(end).reshape(rows // span, width)
    return rise, fall, head, tail, fade


def column_of(table, index):
    lane = lax.broadcasted_iota(jnp.int32, table.shape, 1)
    return jnp.sum(jnp.where(lane == index, table, 0.0), axis=1, keepdims=True)


def norm_of(x):
    return lax.rsqrt(jnp.sum(x * x, axis=1, keepdims=True) + EPS)


def inverse(system, row, col):
    same = row // BASE == col // BASE
    near = jnp.where(same, system, 0.0)
    near_s = split(near)
    square = dot3(near_s, near_s)
    square_s = split(square)
    found = jnp.where(row == col, 1.0, 0.0) - near
    fourth = dot3(square_s, square_s)
    found = found + dot3(split(found), square_s)
    found = found + dot3(split(found), split(fourth))
    block = BASE
    while block < SPAN:
        wide = row // (2 * block) == col // (2 * block)
        off = jnp.where(wide & (row // block != col // block), system, 0.0)
        found_s = split(found)
        found = found - dot3(found_s, split(dot3(split(off), found_s)))
        block *= 2
    return found


def gatherer(n, ins, held, table_ref, table_held, send, recv, own, t_send, t_recv, t_own):
    me = lax.axis_index("head")
    heads, rows, width = held.shape[1:]
    share = rows // n
    mine = pl.ds(pl.multiple_of(me * share, share), share)

    def source(index, h, peer):
        return ins[index].at[:, pl.ds(pl.multiple_of((peer * heads + h) * width, width), width)]

    def local(index, h):
        return pltpu.make_async_copy(source(index, h, me), held.at[index, h, mine], own.at[h, index])

    def remote(index, h, step):
        peer = lax.rem(me + step, n)
        return pltpu.make_async_remote_copy(
            src_ref=source(index, h, peer), dst_ref=held.at[index, h, mine], send_sem=send.at[h, index, step],
            recv_sem=recv.at[h, index, step], device_id={"head": peer}, device_id_type=MESH,
        )

    def table_local():
        return pltpu.make_async_copy(table_ref, table_held.at[mine], t_own)

    def table_remote(step):
        return pltpu.make_async_remote_copy(
            src_ref=table_ref, dst_ref=table_held.at[mine], send_sem=t_send.at[step],
            recv_sem=t_recv.at[step], device_id={"head": lax.rem(me + step, n)}, device_id_type=MESH,
        )

    def start():
        for step in range(1, n):
            table_remote(step).start()

        def start_remote(h, carry):
            for index in range(len(ins)):
                for step in range(1, n):
                    remote(index, h, step).start()
            return carry

        lax.fori_loop(0, heads, start_remote, 0)
        table_local().start()

        def start_local(h, carry):
            for index in range(len(ins)):
                local(index, h).start()
            return carry

        lax.fori_loop(0, heads, start_local, 0)
        table_local().wait()
        for step in range(1, n):
            table_remote(step).wait_recv()

    def arrive(h):
        for index in range(len(ins)):
            local(index, h).wait()
            for step in range(1, n):
                remote(index, h, step).wait_recv()

    def finish():
        for step in range(1, n):
            table_remote(step).wait_send()

        def finish_head(h, carry):
            for index in range(len(ins)):
                for step in range(1, n):
                    remote(index, h, step).wait_send()
            return carry

        lax.fori_loop(0, heads, finish_head, 0)

    return start, arrive, finish


def local_part(h, span, held, table_held, saved, total_ref):
    ev_ref, ek_ref, inv_ref, a_ref, sc_ref, tr_ref, bs_ref, gs_ref = saved
    heads, rows, width = held.shape[1:]
    spans = rows // span
    k, g, q, v, o = (held[index, h] for index in range(5))
    q = q.astype(F32)
    k = k.astype(F32)
    beta = column_of(table_held[...].astype(F32), lax.axis_index("head") * heads + h)
    rise, fall, head, tail, fade = gates(g, span)
    q_unit = q * norm_of(q) * width ** (-0.5)
    k_unit = k * norm_of(k)
    row, col = grids(rows)
    inside = row // span == col // span
    k_fall_s = split(k_unit * fall)
    inner = jnp.where(inside & (col < row), dot3(split(k_unit * rise), k_fall_s, NT), 0.0)
    scores = jnp.where(inside & (col <= row), dot3(split(q_unit * rise), k_fall_s, NT), 0.0)
    a_ref[h] = inner
    sc_ref[h] = scores
    beta_row = jnp.sum(jnp.where(row == col, beta, 0.0), axis=0, keepdims=True)
    found = inverse(inner * beta_row, row, col)
    inv_ref[h] = found
    found_s = split(found)
    e_value = dot3(found_s, v)
    e_key = dot3(found_s, split(k_unit * head))
    ev_ref[h] = e_value
    ek_ref[h] = e_key
    w_key_s = split(e_key * beta)
    w_value_s = split(e_value * beta)
    reach = q_unit * head - dot3(split(scores), w_key_s)
    k_tail = k_unit * tail
    small_row, small_col = grids(width)
    diagonal = small_row == small_col
    moves, adds, backs = [], [], []
    for index in range(spans):
        at = index * span
        tail_t = split(k_tail[at : at + span].T)
        move = jnp.where(diagonal, fade[index : index + 1], 0.0) - dot3(tail_t, rows_of(w_key_s, at, span))
        add = dot3(tail_t, rows_of(w_value_s, at, span))
        back = dot3(split(reach[at : at + span].T), o[at : at + span])
        tr_ref[h, index] = move
        bs_ref[h, index] = add
        gs_ref[h, index] = back
        moves.append(move)
        adds.append(add)
        backs.append(back)
    trans, ends = moves[0], adds[0]
    grad = backs[spans - 1]
    for index in range(1, spans):
        move_s = split(moves[index])
        trans = dot3(move_s, split(trans))
        ends = dot3(move_s, split(ends)) + adds[index]
        mirror = spans - 1 - index
        grad = dot3(split(moves[mirror].T), split(grad)) + backs[mirror]
    total_ref[0, h, 0], total_ref[0, h, 1], total_ref[0, h, 2] = trans, ends, grad


def returner(n, done, db_done, outs, db_out, send, recv, own, t_send, t_recv, t_own):
    me = lax.axis_index("head")
    heads, rows, width = done.shape[1:]
    share = rows // n

    def part(peer):
        return pl.ds(pl.multiple_of(peer * share, share), share)

    def target(index, h):
        return outs[index].at[:, pl.ds(pl.multiple_of((me * heads + h) * width, width), width)]

    def local(index, h):
        return pltpu.make_async_copy(done.at[index, h, part(me)], target(index, h), own.at[h, index])

    def remote(index, h, step):
        peer = lax.rem(me + step, n)
        return pltpu.make_async_remote_copy(
            src_ref=done.at[index, h, part(peer)], dst_ref=target(index, h), send_sem=send.at[h, index, step],
            recv_sem=recv.at[h, index, step], device_id={"head": peer}, device_id_type=MESH,
        )

    def table_local():
        return pltpu.make_async_copy(db_done.at[part(me)], db_out.at[me], t_own)

    def table_remote(step):
        peer = lax.rem(me + step, n)
        return pltpu.make_async_remote_copy(
            src_ref=db_done.at[part(peer)], dst_ref=db_out.at[me], send_sem=t_send.at[step],
            recv_sem=t_recv.at[step], device_id={"head": peer}, device_id_type=MESH,
        )

    def emit(index, h, value):
        done[index, h] = value.astype(BF16)
        local(index, h).start()
        for step in range(1, n):
            remote(index, h, step).start()

    def finish():
        table_local().start()
        for step in range(1, n):
            table_remote(step).start()

        def finish_head(h, carry):
            for index in range(len(outs)):
                local(index, h).wait()
                for step in range(1, n):
                    remote(index, h, step).wait()
            return carry

        lax.fori_loop(0, heads, finish_head, 0)
        table_local().wait()
        for step in range(1, n):
            table_remote(step).wait()

    return emit, finish


def grad_part(h, span, held, table_held, saved, state_ref, dstate_ref, db_all, emit_head):
    ev_ref, ek_ref, inv_ref, a_ref, sc_ref, tr_ref, bs_ref, gs_ref = saved
    heads, rows, width = held.shape[1:]
    spans = rows // span
    k, g, q, _, o = (held[index, h] for index in range(5))
    q = q.astype(F32)
    k = k.astype(F32)
    beta = column_of(table_held[...].astype(F32), lax.axis_index("head") * heads + h)

    def emit(index, value):
        emit_head(index, h, value)

    rise, fall, head, tail, fade = gates(g, span)
    q_norm = norm_of(q)
    k_norm = norm_of(k)
    q_unit = q * q_norm * width ** (-0.5)
    k_unit = k * k_norm
    row, col = grids(rows)
    inside = row // span == col // span
    states = [state_ref[h]]
    grads = [dstate_ref[h]]
    for index in range(spans - 1):
        states.append(dot3(split(tr_ref[h, index]), split(states[-1])) + bs_ref[h, index])
        mirror = spans - 1 - index
        grads.insert(0, dot3(split(tr_ref[h, mirror].T), split(grads[0])) + gs_ref[h, mirror])
    states_s = [split(x) for x in states]
    grads_s = [split(x) for x in grads]

    def each(fn):
        return jnp.concatenate([fn(index, index * span) for index in range(spans)], axis=0)

    ek_s = split(ek_ref[h])
    k_tail = k_unit * tail
    k_tail_s = split(k_tail)
    error = ev_ref[h] - each(lambda i, at: dot3(rows_of(ek_s, at, span), states_s[i]))
    update_s = split(error * beta)
    d_update = dot3(split(sc_ref[h].T), o) + each(lambda i, at: dot3(rows_of(k_tail_s, at, span), grads_s[i]))
    d_value = dot3(split(inv_ref[h].T), split(d_update * beta))
    d_value_s = split(d_value)
    emit(0, d_value)
    residue = d_update - dot3(split(a_ref[h].T), d_value_s)
    d_beta = jnp.sum(error * residue, axis=1, keepdims=True)
    lane = lax.broadcasted_iota(jnp.int32, db_all.shape, 1)
    db_all[...] = jnp.where(lane == h, d_beta, db_all[...])
    dq_head = each(lambda i, at: dot3(o[at : at + span], states_s[i], NT))
    dk_head = -each(lambda i, at: dot3(rows_of(d_value_s, at, span), states_s[i], NT))
    dk_tail = each(lambda i, at: dot3(rows_of(update_s, at, span), grads_s[i], NT))
    d_scores = jnp.where(inside & (col <= row), dot3(o, update_s, NT), 0.0)
    d_inner = jnp.where(inside & (col < row), -dot3(d_value_s, update_s, NT), 0.0)
    k_fall_s = split(k_unit * fall)
    dq_rise = dot3(split(d_scores), k_fall_s)
    dk_rise = dot3(split(d_inner), k_fall_s)
    dk_fall = dot3(split(d_scores.T), split(q_unit * rise)) + dot3(split(d_inner.T), split(k_unit * rise))
    dq_unit = dq_rise * rise + dq_head * head
    up = dk_rise * rise + dk_head * head
    tail_part = dk_tail * tail
    down = dk_fall * fall + tail_part
    d_gamma = q_unit * dq_unit + k_unit * (up - down)
    tail_sum = jnp.sum((k_unit * tail_part).reshape(spans, span, width), axis=1, keepdims=True)
    small_row, small_col = grids(width)
    diagonal = small_row == small_col
    last = []
    for index in range(spans):
        d_fade = jnp.sum(states[index] * grads[index], axis=1, keepdims=True)
        d_fade = jnp.sum(jnp.where(diagonal, d_fade, 0.0), axis=0, keepdims=True)
        last.append(d_fade * fade[index : index + 1])
    last = jnp.concatenate([x.reshape(1, 1, width) for x in last], axis=0)
    sum_mask = jnp.where(inside & (col >= row), 1.0, 0.0).astype(BF16)
    d_decay = dot3(sum_mask, split(d_gamma)) + per_span(tail_sum + last, span, d_gamma)
    scale = width ** (-0.5)
    dq = (dq_unit - q * (q_norm * q_norm * jnp.sum(q * dq_unit, axis=1, keepdims=True))) * (q_norm * scale)
    emit(1, dq)
    dk_unit = up + down
    dk = (dk_unit - k * (k_norm * k_norm * jnp.sum(k * dk_unit, axis=1, keepdims=True))) * k_norm
    emit(2, dk)
    emit(3, d_decay)


def exchanger(total_ref, other_ref, send, recv):
    me = lax.axis_index("ctx")

    def partner(r):
        bit = 2**r
        return me + bit - 2 * bit * lax.rem(me // bit, 2)

    def swap(r, h):
        return pltpu.make_async_remote_copy(
            src_ref=total_ref.at[r, h], dst_ref=other_ref.at[r, h], send_sem=send.at[r, h],
            recv_sem=recv.at[r, h], device_id={"ctx": partner(r)}, device_id_type=MESH,
        )

    return partner, swap


def combine(r, rounds, h, total_ref, other_ref, lead_ref, trail_ref, state_ref, dstate_ref):
    upper = lax.rem(lax.axis_index("ctx") // 2**r, 2) == 1
    trans, ends, grad = (total_ref.at[r, h, index] for index in range(3))
    other, other_ends, other_grad = (other_ref.at[r, h, index] for index in range(3))
    more = r < rounds - 1

    @pl.when(upper)
    def _():
        other_s, ends_s = split(other[...]), split(other_ends[...])
        lead_s = split(lead_ref[h])
        state_ref[h] = state_ref[h] + dot3(lead_s, ends_s)
        if more:
            lead_ref[h] = dot3(lead_s, other_s)
            trans_s = split(trans[...])
            total_ref[r + 1, h, 0] = dot3(trans_s, other_s)
            total_ref[r + 1, h, 1] = dot3(trans_s, ends_s) + ends[...]
            total_ref[r + 1, h, 2] = other_grad[...] + dot3(split(other[...].T), split(grad[...]))

    @pl.when(jnp.logical_not(upper))
    def _():
        grad_s = split(other_grad[...])
        trail_s = split(trail_ref[h])
        dstate_ref[h] = dstate_ref[h] + dot3(trail_s, grad_s)
        if more:
            other_s = split(other[...])
            trail_ref[h] = dot3(trail_s, other_s, NT)
            trans_s = split(trans[...])
            total_ref[r + 1, h, 0] = dot3(other_s, trans_s)
            total_ref[r + 1, h, 1] = dot3(other_s, split(ends[...])) + other_ends[...]
            total_ref[r + 1, h, 2] = grad[...] + dot3(split(trans[...].T), grad_s)


def layer_kernel(n, rounds, span, q_ref, k_ref, v_ref, g_ref, o_ref, b_ref, dq_out, dk_out, dv_out, dg_out, db_out,
                 held, table_held, done, db_all, db_done, ev, ek, inv, a, sc, tr, bs, gs, total, other, lead, trail,
                 state, dstate, x_send, x_recv, *semaphores):
    t = pl.program_id(0)
    heads, width = held.shape[1], held.shape[3]
    saved = (ev, ek, inv, a, sc, tr, bs, gs)
    start, arrive, finish_in = gatherer(
        n, (k_ref, g_ref, q_ref, v_ref, o_ref), held, b_ref, table_held, *semaphores[:6]
    )
    emit, finish_out = returner(n, done, db_done, (dv_out, dq_out, dk_out, dg_out), db_out, *semaphores[6:])
    partner, swap = exchanger(total, other, x_send, x_recv)

    @pl.when(t == 0)
    def _():
        me = lax.axis_index("head")
        barrier = pltpu.get_barrier_semaphore()
        for step in range(1, n):
            pl.semaphore_signal(
                barrier, inc=1, device_id={"head": lax.rem(me + step, n)}, device_id_type=MESH
            )
        for r in range(rounds):
            pl.semaphore_signal(barrier, inc=1, device_id={"ctx": partner(r)}, device_id_type=MESH)
        db_all[...] = jnp.zeros_like(db_all)
        state[...] = jnp.zeros_like(state)
        dstate[...] = jnp.zeros_like(dstate)
        row, col = grids(width)
        unit = jnp.where(row == col, 1.0, 0.0)
        for h in range(heads):
            lead[h] = unit
            trail[h] = unit
        pl.semaphore_wait(barrier, n - 1 + rounds)
        start()

    def turn(r):
        h = t - 1 - r

        @pl.when((h >= 0) & (h < heads))
        def _():
            swap(r, h).wait_recv()
            combine(r, rounds, h, total, other, lead, trail, state, dstate)
            if r < rounds - 1:
                swap(r + 1, h).start()

    for r in range(rounds - 1, 0, -1):
        turn(r)

    if rounds == 1:
        turn(0)

    @pl.when(t >= rounds)
    def _():
        grad_part(t - rounds, span, held, table_held, saved, state, dstate, db_all, emit)

    if rounds > 1:
        turn(0)

    @pl.when(t < heads)
    def _():
        arrive(t)
        local_part(t, span, held, table_held, saved, total)
        swap(0, t).start()

    @pl.when(t == heads + rounds - 1)
    def _():
        db_done[...] = db_all[...].astype(BF16)
        finish_out()
        finish_in()

        def finish_swap(h, carry):
            for r in range(rounds):
                swap(r, h).wait_send()
            return carry

        lax.fori_loop(0, heads, finish_swap, 0)


def per_device(queries, key_in, values_in, strength, log_decay, d_out):
    heads_all = strength.shape[1]
    n = lax.axis_size("head")
    rounds = lax.axis_size("ctx").bit_length() - 1
    heads = heads_all // n
    width = queries.shape[1] // heads_all
    share = queries.shape[0]
    rows = n * share
    spans = rows // SPAN
    outside = pl.BlockSpec(memory_space=pl.ANY)
    full_t = jax.ShapeDtypeStruct(queries.shape, BF16)
    dma = pltpu.SemaphoreType.DMA
    vmem = pltpu.VMEM

    def semaphores(count):
        return [dma((heads, count, n))] * 2 + [dma((heads, count))] + [dma((n,))] * 2 + [dma(())]

    narrow = vmem((heads, rows, width), F32)
    square = vmem((heads, rows, rows), F32)
    state = vmem((heads, width, width), F32)
    state_list = vmem((heads, spans, width, width), F32)
    totals = vmem((rounds, heads, 3, width, width), F32)
    dq, dk, dv, dg, ds = pl.pallas_call(
        functools.partial(layer_kernel, n, rounds, SPAN),
        grid=(heads + rounds,),
        in_specs=[outside] * 6,
        out_specs=[outside] * 5,
        out_shape=[full_t] * 4 + [jax.ShapeDtypeStruct((n, share, heads), BF16)],
        scratch_shapes=[
            vmem((5, heads, rows, width), BF16), vmem((rows, heads_all), BF16),
            vmem((4, heads, rows, width), BF16), vmem((rows, heads), F32), vmem((rows, heads), BF16),
        ] + [narrow] * 2 + [square] * 3 + [state_list] * 3 + [totals] * 2 + [state] * 4
        + [dma((rounds, heads))] * 2 + semaphores(5) + semaphores(4),
        compiler_params=pltpu.CompilerParams(
            dimension_semantics=("arbitrary",), vmem_limit_bytes=60 * 1024 * 1024,
            collective_id=0, has_side_effects=True,
        ),
        name="layer",
    )(queries, key_in, values_in, log_decay, d_out, strength)
    return dq, dk, dv, jnp.transpose(ds, (1, 0, 2)).reshape(share, heads_all), dg


def solution(mesh):
    spec = P(("ctx", "head"), None)
    return jax.shard_map(
        per_device, mesh=mesh, in_specs=(spec,) * 6, out_specs=(spec,) * 5, check_vma=False
    )
```

```python
import functools

import jax
import jax.numpy as jnp
from jax import lax
from jax.experimental import pallas as pl
from jax.experimental.pallas import tpu as pltpu
from jax.sharding import PartitionSpec as P

SPAN = 64
BASE = 8
EPS = 1e-06
F32 = jnp.float32
BF16 = jnp.bfloat16
MESH = pl.DeviceIdType.MESH

NN = (((1,), (0,)), ((), ()))
NT = (((1,), (1,)), ((), ()))


def split(x):
    high = x.astype(BF16)
    return high, (x - high.astype(F32)).astype(BF16)


def mul(a, b, dims=NN):
    return lax.dot_general(a, b, dims, preferred_element_type=F32)


def dot3(a, b, dims=NN):
    if not isinstance(a, tuple):
        return mul(a, b[0], dims) + mul(a, b[1], dims)
    if not isinstance(b, tuple):
        return mul(a[0], b, dims) + mul(a[1], b, dims)
    return mul(a[0], b[0], dims) + (mul(a[0], b[1], dims) + mul(a[1], b[0], dims))


def rows_of(pair, start, size):
    if not isinstance(pair, tuple):
        return pair[start : start + size]
    return tuple(part[start : start + size] for part in pair)


def both(a, b, axis):
    return tuple(jnp.concatenate([x, y], axis=axis) for x, y in zip(a, b))


def grids(size):
    return (
        lax.broadcasted_iota(jnp.int32, (size, size), 0),
        lax.broadcasted_iota(jnp.int32, (size, size), 1),
    )


def per_span(row_values, span, like):
    rows, width = like.shape
    return jnp.broadcast_to(row_values, (rows // span, span, width)).reshape(rows, width)


def gates(g, span):
    rows, width = g.shape
    row, col = grids(rows)
    sum_mask = jnp.where((row // span == col // span) & (col <= row), 1.0, 0.0).astype(BF16)
    gamma = mul(sum_mask, g)
    spans = gamma.reshape(rows // span, span, width)
    middle = spans[:, span // 2 - 1 : span // 2]
    end = spans[:, span - 1 : span]
    centred = gamma - per_span(middle, span, gamma)
    rise = jnp.exp(centred)
    fall = jnp.exp(-centred)
    head = rise * per_span(jnp.exp(middle), span, gamma)
    tail = fall * per_span(jnp.exp(end - middle), span, gamma)
    fade = jnp.exp(end).reshape(rows // span, width)
    return rise, fall, head, tail, fade


def column_of(table, index):
    parts, heads, share = table.shape
    row, col = grids(share)
    head = lax.broadcasted_iota(jnp.int32, (heads, share), 0)
    lines = [jnp.sum(jnp.where(head == index, table[p], 0.0), axis=0, keepdims=True) for p in range(parts)]
    return jnp.concatenate(
        [jnp.sum(jnp.where(row == col, line, 0.0), axis=1, keepdims=True) for line in lines], axis=0
    )


def norm_of(x):
    return lax.rsqrt(jnp.sum(x * x, axis=1, keepdims=True) + EPS)


def inverse(system, row, col):
    same = row // BASE == col // BASE
    near = jnp.where(same, system, 0.0)
    near_s = split(near)
    square = dot3(near_s, near_s)
    square_s = split(square)
    found = jnp.where(row == col, 1.0, 0.0) - near
    fourth = dot3(square_s, square_s)
    found = found + dot3(split(found), square_s)
    found = found + dot3(split(found), split(fourth))
    block = BASE
    while block < SPAN:
        wide = row // (2 * block) == col // (2 * block)
        off = jnp.where(wide & (row // block != col // block), system, 0.0)
        found_s = split(found)
        found = found - dot3(found_s, split(dot3(split(off), found_s)))
        block *= 2
    return found


def gatherer(n, ins, held, table_ref, table_held, send, recv, own, t_send, t_recv, t_own):
    me = lax.axis_index("head")
    heads, rows, width = held.shape[1:]
    share = rows // n
    mine = pl.ds(pl.multiple_of(me * share, share), share)

    def source(index, h, peer):
        return ins[index].at[:, pl.ds(pl.multiple_of((peer * heads + h) * width, width), width)]

    def local(index, h):
        return pltpu.make_async_copy(source(index, h, me), held.at[index, h, mine], own.at[h, index])

    def remote(index, h, step):
        peer = lax.rem(me + step, n)
        return pltpu.make_async_remote_copy(
            src_ref=source(index, h, peer), dst_ref=held.at[index, h, mine], send_sem=send.at[h, index, step],
            recv_sem=recv.at[h, index, step], device_id={"head": peer}, device_id_type=MESH,
        )

    def table_local():
        return pltpu.make_async_copy(table_ref, table_held.at[me], t_own)

    def table_remote(step):
        return pltpu.make_async_remote_copy(
            src_ref=table_ref, dst_ref=table_held.at[me], send_sem=t_send.at[step],
            recv_sem=t_recv.at[step], device_id={"head": lax.rem(me + step, n)}, device_id_type=MESH,
        )

    def start():
        for step in range(1, n):
            table_remote(step).start()

        def start_remote(h, carry):
            for index in range(len(ins)):
                for step in range(1, n):
                    remote(index, h, step).start()
            return carry

        lax.fori_loop(0, heads, start_remote, 0)
        table_local().start()

        def start_local(h, carry):
            for index in range(len(ins)):
                local(index, h).start()
            return carry

        lax.fori_loop(0, heads, start_local, 0)
        table_local().wait()
        for step in range(1, n):
            table_remote(step).wait_recv()

    def arrive(h):
        for index in range(len(ins)):
            local(index, h).wait()
            for step in range(1, n):
                remote(index, h, step).wait_recv()

    def finish():
        for step in range(1, n):
            table_remote(step).wait_send()

        def finish_head(h, carry):
            for index in range(len(ins)):
                for step in range(1, n):
                    remote(index, h, step).wait_send()
            return carry

        lax.fori_loop(0, heads, finish_head, 0)

    return start, arrive, finish


def local_part(h, span, held, table_held, saved, total_ref):
    ev_ref, ek_ref, inv_ref, a_ref, sc_ref, tr_ref, bs_ref, gs_ref = saved
    heads, rows, width = held.shape[1:]
    spans = rows // span
    k, g, q, v, o = (held[index, h] for index in range(5))
    q = q.astype(F32)
    k = k.astype(F32)
    beta = column_of(table_held[...].astype(F32), lax.axis_index("head") * heads + h)
    rise, fall, head, tail, fade = gates(g, span)
    q_unit = q * norm_of(q) * width ** (-0.5)
    k_unit = k * norm_of(k)
    row, col = grids(rows)
    inside = row // span == col // span
    k_fall_s = split(k_unit * fall)
    inner = jnp.where(inside & (col < row), dot3(split(k_unit * rise), k_fall_s, NT), 0.0)
    scores = jnp.where(inside & (col <= row), dot3(split(q_unit * rise), k_fall_s, NT), 0.0)
    a_ref[h] = inner
    sc_ref[h] = scores
    beta_row = jnp.sum(jnp.where(row == col, beta, 0.0), axis=0, keepdims=True)
    found = inverse(inner * beta_row, row, col)
    inv_ref[h] = found
    found_s = split(found)
    e_value = dot3(found_s, v)
    e_key = dot3(found_s, split(k_unit * head))
    ev_ref[h] = e_value
    ek_ref[h] = e_key
    w_key_s = split(e_key * beta)
    w_value_s = split(e_value * beta)
    reach = q_unit * head - dot3(split(scores), w_key_s)
    k_tail = k_unit * tail
    small_row, small_col = grids(width)
    diagonal = small_row == small_col
    moves, adds, backs = [], [], []
    for index in range(spans):
        at = index * span
        tail_t = split(k_tail[at : at + span].T)
        move = jnp.where(diagonal, fade[index : index + 1], 0.0) - dot3(tail_t, rows_of(w_key_s, at, span))
        add = dot3(tail_t, rows_of(w_value_s, at, span))
        back = dot3(split(reach[at : at + span].T), o[at : at + span])
        tr_ref[h, index] = move
        bs_ref[h, index] = add
        gs_ref[h, index] = back
        moves.append(move)
        adds.append(add)
        backs.append(back)
    trans, ends = moves[0], adds[0]
    grad = backs[spans - 1]
    for index in range(1, spans):
        move_s = split(moves[index])
        trans = dot3(move_s, split(trans))
        ends = dot3(move_s, split(ends)) + adds[index]
        mirror = spans - 1 - index
        grad = dot3(split(moves[mirror].T), split(grad)) + backs[mirror]
    total_ref[0, h, 0], total_ref[0, h, 1], total_ref[0, h, 2] = trans, ends, grad


def returner(n, done, db_done, outs, db_out, send, recv, own, t_send, t_recv, t_own):
    me = lax.axis_index("head")
    heads, rows, width = done.shape[1:]
    share = rows // n

    def part(peer):
        return pl.ds(pl.multiple_of(peer * share, share), share)

    def target(index, h):
        return outs[index].at[:, pl.ds(pl.multiple_of((me * heads + h) * width, width), width)]

    def local(index, h):
        return pltpu.make_async_copy(done.at[index, h, part(me)], target(index, h), own.at[h, index])

    def remote(index, h, step):
        peer = lax.rem(me + step, n)
        return pltpu.make_async_remote_copy(
            src_ref=done.at[index, h, part(peer)], dst_ref=target(index, h), send_sem=send.at[h, index, step],
            recv_sem=recv.at[h, index, step], device_id={"head": peer}, device_id_type=MESH,
        )

    def table_local():
        return pltpu.make_async_copy(db_done.at[me], db_out.at[me], t_own)

    def table_remote(step):
        peer = lax.rem(me + step, n)
        return pltpu.make_async_remote_copy(
            src_ref=db_done.at[peer], dst_ref=db_out.at[me], send_sem=t_send.at[step],
            recv_sem=t_recv.at[step], device_id={"head": peer}, device_id_type=MESH,
        )

    def emit(index, h, value):
        done[index, h] = value.astype(BF16)
        local(index, h).start()
        for step in range(1, n):
            remote(index, h, step).start()

    def finish():
        table_local().start()
        for step in range(1, n):
            table_remote(step).start()

        def finish_head(h, carry):
            for index in range(len(outs)):
                local(index, h).wait()
                for step in range(1, n):
                    remote(index, h, step).wait()
            return carry

        lax.fori_loop(0, heads, finish_head, 0)
        table_local().wait()
        for step in range(1, n):
            table_remote(step).wait()

    return emit, finish


def grad_part(h, span, held, table_held, saved, state_ref, dstate_ref, db_all, emit_head):
    ev_ref, ek_ref, inv_ref, a_ref, sc_ref, tr_ref, bs_ref, gs_ref = saved
    heads, rows, width = held.shape[1:]
    spans = rows // span
    k, g, q, _, o = (held[index, h] for index in range(5))
    q = q.astype(F32)
    k = k.astype(F32)
    beta = column_of(table_held[...].astype(F32), lax.axis_index("head") * heads + h)

    def emit(index, value):
        emit_head(index, h, value)

    rise, fall, head, tail, fade = gates(g, span)
    q_norm = norm_of(q)
    k_norm = norm_of(k)
    q_unit = q * q_norm * width ** (-0.5)
    k_unit = k * k_norm
    row, col = grids(rows)
    inside = row // span == col // span
    states = [state_ref[h]]
    grads = [dstate_ref[h]]
    for index in range(spans - 1):
        states.append(dot3(split(tr_ref[h, index]), split(states[-1])) + bs_ref[h, index])
        mirror = spans - 1 - index
        grads.insert(0, dot3(split(tr_ref[h, mirror].T), split(grads[0])) + gs_ref[h, mirror])
    states_s = [split(x) for x in states]
    grads_s = [split(x) for x in grads]

    def each(fn):
        return jnp.concatenate([fn(index, index * span) for index in range(spans)], axis=0)

    ek_s = split(ek_ref[h])
    k_tail = k_unit * tail
    k_tail_s = split(k_tail)
    error = ev_ref[h] - each(lambda i, at: dot3(rows_of(ek_s, at, span), states_s[i]))
    update_s = split(error * beta)
    d_update = dot3(split(sc_ref[h].T), o) + each(lambda i, at: dot3(rows_of(k_tail_s, at, span), grads_s[i]))
    d_value = dot3(split(inv_ref[h].T), split(d_update * beta))
    d_value_s = split(d_value)
    emit(0, d_value)
    residue = d_update - dot3(split(a_ref[h].T), d_value_s)
    d_beta = jnp.sum(error * residue, axis=1, keepdims=True)
    parts, _, share = db_all.shape
    at_row, at_col = grids(share)
    sublane = lax.broadcasted_iota(jnp.int32, (heads, share), 0)
    for p in range(parts):
        piece = d_beta[p * share : (p + 1) * share]
        line = jnp.sum(jnp.where(at_row == at_col, piece, 0.0), axis=0, keepdims=True)
        db_all[p] = jnp.where(sublane == h, line, db_all[p])
    dq_head = each(lambda i, at: dot3(o[at : at + span], states_s[i], NT))
    dk_head = -each(lambda i, at: dot3(rows_of(d_value_s, at, span), states_s[i], NT))
    dk_tail = each(lambda i, at: dot3(rows_of(update_s, at, span), grads_s[i], NT))
    d_scores = jnp.where(inside & (col <= row), dot3(o, update_s, NT), 0.0)
    d_inner = jnp.where(inside & (col < row), -dot3(d_value_s, update_s, NT), 0.0)
    k_fall_s = split(k_unit * fall)
    dq_rise = dot3(split(d_scores), k_fall_s)
    dk_rise = dot3(split(d_inner), k_fall_s)
    dk_fall = dot3(split(d_scores.T), split(q_unit * rise)) + dot3(split(d_inner.T), split(k_unit * rise))
    dq_unit = dq_rise * rise + dq_head * head
    up = dk_rise * rise + dk_head * head
    tail_part = dk_tail * tail
    down = dk_fall * fall + tail_part
    d_gamma = q_unit * dq_unit + k_unit * (up - down)
    tail_sum = jnp.sum((k_unit * tail_part).reshape(spans, span, width), axis=1, keepdims=True)
    small_row, small_col = grids(width)
    diagonal = small_row == small_col
    last = []
    for index in range(spans):
        d_fade = jnp.sum(states[index] * grads[index], axis=1, keepdims=True)
        d_fade = jnp.sum(jnp.where(diagonal, d_fade, 0.0), axis=0, keepdims=True)
        last.append(d_fade * fade[index : index + 1])
    last = jnp.concatenate([x.reshape(1, 1, width) for x in last], axis=0)
    sum_mask = jnp.where(inside & (col >= row), 1.0, 0.0).astype(BF16)
    d_decay = dot3(sum_mask, split(d_gamma)) + per_span(tail_sum + last, span, d_gamma)
    scale = width ** (-0.5)
    dq = (dq_unit - q * (q_norm * q_norm * jnp.sum(q * dq_unit, axis=1, keepdims=True))) * (q_norm * scale)
    emit(1, dq)
    dk_unit = up + down
    dk = (dk_unit - k * (k_norm * k_norm * jnp.sum(k * dk_unit, axis=1, keepdims=True))) * k_norm
    emit(2, dk)
    emit(3, d_decay)


def exchanger(total_ref, other_ref, send, recv):
    me = lax.axis_index("ctx")

    def partner(r):
        bit = 2**r
        return me + bit - 2 * bit * lax.rem(me // bit, 2)

    def swap(r, h):
        return pltpu.make_async_remote_copy(
            src_ref=total_ref.at[r, h], dst_ref=other_ref.at[r, h], send_sem=send.at[r, h],
            recv_sem=recv.at[r, h], device_id={"ctx": partner(r)}, device_id_type=MESH,
        )

    return partner, swap


def combine(r, rounds, h, total_ref, other_ref, lead_ref, trail_ref, state_ref, dstate_ref):
    upper = lax.rem(lax.axis_index("ctx") // 2**r, 2) == 1
    trans, ends, grad = (total_ref.at[r, h, index] for index in range(3))
    other, other_ends, other_grad = (other_ref.at[r, h, index] for index in range(3))
    more = r < rounds - 1

    @pl.when(upper)
    def _():
        other_s, ends_s = split(other[...]), split(other_ends[...])
        lead_s = split(lead_ref[h])
        state_ref[h] = state_ref[h] + dot3(lead_s, ends_s)
        if more:
            lead_ref[h] = dot3(lead_s, other_s)
            trans_s = split(trans[...])
            total_ref[r + 1, h, 0] = dot3(trans_s, other_s)
            total_ref[r + 1, h, 1] = dot3(trans_s, ends_s) + ends[...]
            total_ref[r + 1, h, 2] = other_grad[...] + dot3(split(other[...].T), split(grad[...]))

    @pl.when(jnp.logical_not(upper))
    def _():
        grad_s = split(other_grad[...])
        trail_s = split(trail_ref[h])
        dstate_ref[h] = dstate_ref[h] + dot3(trail_s, grad_s)
        if more:
            other_s = split(other[...])
            trail_ref[h] = dot3(trail_s, other_s, NT)
            trans_s = split(trans[...])
            total_ref[r + 1, h, 0] = dot3(other_s, trans_s)
            total_ref[r + 1, h, 1] = dot3(other_s, split(ends[...])) + other_ends[...]
            total_ref[r + 1, h, 2] = grad[...] + dot3(split(trans[...].T), grad_s)


def layer_kernel(n, rounds, span, q_ref, k_ref, v_ref, g_ref, o_ref, b_ref, dq_out, dk_out, dv_out, dg_out, db_out,
                 held, table_held, done, db_all, db_done, ev, ek, inv, a, sc, tr, bs, gs, total, other, lead, trail,
                 state, dstate, x_send, x_recv, *semaphores):
    t = pl.program_id(0)
    heads, width = held.shape[1], held.shape[3]
    saved = (ev, ek, inv, a, sc, tr, bs, gs)
    start, arrive, finish_in = gatherer(
        n, (k_ref, g_ref, q_ref, v_ref, o_ref), held, b_ref, table_held, *semaphores[:6]
    )
    emit, finish_out = returner(n, done, db_done, (dv_out, dq_out, dk_out, dg_out), db_out, *semaphores[6:])
    partner, swap = exchanger(total, other, x_send, x_recv)

    @pl.when(t == 0)
    def _():
        me = lax.axis_index("head")
        barrier = pltpu.get_barrier_semaphore()
        for step in range(1, n):
            pl.semaphore_signal(
                barrier, inc=1, device_id={"head": lax.rem(me + step, n)}, device_id_type=MESH
            )
        for r in range(rounds):
            pl.semaphore_signal(barrier, inc=1, device_id={"ctx": partner(r)}, device_id_type=MESH)
        db_all[...] = jnp.zeros_like(db_all)
        state[...] = jnp.zeros_like(state)
        dstate[...] = jnp.zeros_like(dstate)
        row, col = grids(width)
        unit = jnp.where(row == col, 1.0, 0.0)
        for h in range(heads):
            lead[h] = unit
            trail[h] = unit
        pl.semaphore_wait(barrier, n - 1 + rounds)
        start()

    def turn(r):
        h = t - 1 - r

        @pl.when((h >= 0) & (h < heads))
        def _():
            swap(r, h).wait_recv()
            combine(r, rounds, h, total, other, lead, trail, state, dstate)
            if r < rounds - 1:
                swap(r + 1, h).start()

    for r in range(rounds - 1, 0, -1):
        turn(r)

    if rounds == 1:
        turn(0)

    @pl.when(t >= rounds)
    def _():
        grad_part(t - rounds, span, held, table_held, saved, state, dstate, db_all, emit)

    if rounds > 1:
        turn(0)

    @pl.when(t < heads)
    def _():
        arrive(t)
        local_part(t, span, held, table_held, saved, total)
        swap(0, t).start()

    @pl.when(t == heads + rounds - 1)
    def _():
        db_done[...] = db_all[...].astype(BF16)
        finish_out()
        finish_in()

        def finish_swap(h, carry):
            for r in range(rounds):
                swap(r, h).wait_send()
            return carry

        lax.fori_loop(0, heads, finish_swap, 0)


def per_device(queries, key_in, values_in, strength, log_decay, d_out):
    heads_all = strength.shape[1]
    n = lax.axis_size("head")
    rounds = lax.axis_size("ctx").bit_length() - 1
    heads = heads_all // n
    width = queries.shape[1] // heads_all
    share = queries.shape[0]
    rows = n * share
    spans = rows // SPAN
    outside = pl.BlockSpec(memory_space=pl.ANY)
    full_t = jax.ShapeDtypeStruct(queries.shape, BF16)
    dma = pltpu.SemaphoreType.DMA
    vmem = pltpu.VMEM

    def semaphores(count):
        return [dma((heads, count, n))] * 2 + [dma((heads, count))] + [dma((n,))] * 2 + [dma(())]

    narrow = vmem((heads, rows, width), F32)
    square = vmem((heads, rows, rows), F32)
    state = vmem((heads, width, width), F32)
    state_list = vmem((heads, spans, width, width), F32)
    totals = vmem((rounds, heads, 3, width, width), F32)
    dq, dk, dv, dg, ds = pl.pallas_call(
        functools.partial(layer_kernel, n, rounds, SPAN),
        grid=(heads + rounds,),
        in_specs=[outside] * 6,
        out_specs=[outside] * 5,
        out_shape=[full_t] * 4 + [jax.ShapeDtypeStruct((n, heads, share), BF16)],
        scratch_shapes=[
            vmem((5, heads, rows, width), BF16), vmem((n, heads_all, share), BF16),
            vmem((4, heads, rows, width), BF16), vmem((n, heads, share), F32), vmem((n, heads, share), BF16),
        ] + [narrow] * 2 + [square] * 3 + [state_list] * 3 + [totals] * 2 + [state] * 4
        + [dma((rounds, heads))] * 2 + semaphores(5) + semaphores(4),
        compiler_params=pltpu.CompilerParams(
            dimension_semantics=("arbitrary",), vmem_limit_bytes=60 * 1024 * 1024,
            collective_id=0, has_side_effects=True,
        ),
        name="layer",
    )(queries, key_in, values_in, log_decay, d_out, strength.T)
    return dq, dk, dv, ds.reshape(heads_all, share).T, dg


def solution(mesh):
    spec = P(("ctx", "head"), None)
    return jax.shard_map(
        per_device, mesh=mesh, in_specs=(spec,) * 6, out_specs=(spec,) * 5, check_vma=False
    )
```
